256 devices in a mesh: dp: 8 (over z), expert: 32 (over y, x, core).
Axes of the slice: x: 4, y: 4, z: 8, core: 2. Of those that a mesh axis runs over, the one named last changes fastest.
Arguments:
- hidden_in: bfloat16 [1024, 5120], P(('dp', 'expert')), may hold values from -6 to 6
- query: bfloat16 [1024, 36864], P(('dp', 'expert')), may hold values from -6 to 24
- prefix_pool: bfloat16 [128, 36864], P('dp'), may hold values from -6 to 6
- suffix_cache: bfloat16 [1024, 73728], P(('dp', 'expert')), may hold values from -6 to 6
- block_list: int32 [1024, 32], P(('dp', 'expert')), may hold values from 0 to 127, as said below
- prefix_count: int32 [1024], P(('dp', 'expert')), may hold values from 1 to 32
- suffix_count: int32 [1024], P(('dp', 'expert')), may hold values from 1 to 128
- value_up: bfloat16 [64, 512, 128], P('expert'), may hold values from -0.25 to 0.25
- out_proj: bfloat16 [8192, 5120], P('expert'), may hold values from -0.5 to 0.5
- norm_gain: bfloat16 [5120], replicated, may hold values from 0.5 to 1.5
- expert_ids: int32 [1024, 6], P(('dp', 'expert')), may hold values from 0 to 31, all different within a row; in each aligned block of 4 rows (0 to 3, 4 to 7, ...) at most 2 rows name the same one
- gate_weights: bfloat16 [1024, 6], P(('dp', 'expert')), may hold values from 0.049804688 to 1
- gate_proj: bfloat16 [32, 5120, 1536], P('expert', None, 'dp'), may hold values from -0.078125 to 0.078125
- up_proj: bfloat16 [32, 5120, 1536], P('expert', None, 'dp'), may hold values from -0.078125 to 0.078125
- down_proj: bfloat16 [32, 1536, 5120], P('expert', 'dp'), may hold values from -0.15625 to 0.15625
Outputs:
- residual_out: float32 [1024, 5120], P(('dp', 'expert'))
- moe_out: float32 [1024, 5120], P(('dp', 'expert'))
The draws below stay inside these ranges and needn't reach their ends.
Inputs may be any that keep to these rules, and one draw needn't show every extreme that they name: `block_list`: each list names 32 distinct blocks; the lists form a prefix tree: two requests with the same block at a position have the same blocks at all earlier positions. `expert_ids`: each row names 6 different experts; among the rows of one device no expert is named more than 2 times.
All inputs are finite; a program needn't handle non-finite values.
Results may differ from the reference program's by a relative error of at most 0.025.
Values may be sent and summed in bfloat16 or wider, within the bound.
A program may use at most 128 MiB of HBM per device.

```python
import math
import jax
import jax.numpy as jnp
import numpy as np
from jax import lax

D = 5120
HEADS = 64
LAT = 512
VH = 128
FF = 1536
TOPK = 6
BLOCK = 64
REQ_DEV = 4
SUFFIX = 128
KDIM = 576
TOKENS = 1024
NBLK = 128
NB = 32
EXPERTS = 32
CAP = 2
FF_GROUP = 192
N_DP = 8


def draw_query(key, part):
    values = jax.random.normal(key, (TOKENS, HEADS, KDIM), jnp.float32)
    values = jnp.clip(values, -6.0, 24.0)
    return values.reshape(TOKENS, HEADS * KDIM).astype(jnp.bfloat16)


def draw_prefix_pool(key, part):
    values = jax.random.normal(key, (NBLK, BLOCK * KDIM), jnp.float32)
    return jnp.clip(values, -6.0, 6.0).astype(jnp.bfloat16)


def draw_suffix_cache(key, part):
    values = jax.random.normal(key, (TOKENS, SUFFIX * KDIM), jnp.float32)
    return jnp.clip(values, -6.0, 6.0).astype(jnp.bfloat16)


def draw_block_list(key, part):
    ordering = jax.random.permutation(jax.random.fold_in(key, 3), NBLK).astype(jnp.int32)
    branch = jax.random.randint(jax.random.fold_in(key, 4), (TOKENS, 1), 0, 4, dtype=jnp.int32)
    levels = jnp.arange(NB, dtype=jnp.int32)[None, :]
    node_index = jnp.where(levels == 0, 0, jnp.where(levels == 1, branch // 2, branch))
    return ordering[levels * 4 + node_index].astype(jnp.int32)


def with_ends(drawn, stream_key, smallest, largest):
    dims = drawn.shape
    index_at = [jax.random.randint(jax.random.fold_in(stream_key, axis), (), 0, dims[axis]) for axis in range(len(dims))]
    drawn = drawn.at[tuple(index_at)].set(smallest)
    longest = dims.index(max(dims))
    index_at[longest] = (index_at[longest] + 1) % dims[longest]
    return drawn.at[tuple(index_at)].set(largest)


def block_levels(rng, shape, shards, least, top_value):
    def one(dim, shards_of):
        steps = jax.random.uniform(jax.random.fold_in(jax.random.fold_in(rng, 6), dim), (shards_of,), jnp.float32, least / len(shards), top_value / len(shards))
        return jnp.repeat(jnp.exp(steps), shape[dim] // shards_of).reshape((-1,) + (1,) * (len(shape) - dim - 1))

    level = one(*shards[0])
    for cut in shards[1:]:
        level = level * one(*cut)
    return level


def routed_block(own_key, own, number, rows, count, top, bound, lean):
    sequence = jax.random.permutation(own_key, count)
    crowded, usual = shares(count, rows * top, bound, lean, True), shares(count, rows * top, bound, lean, False)
    places = jnp.arange(count)

    def named(sizes, turn):
        used = int((sizes > 0).sum())
        fixed = max(1, used // 4)
        passed = fixed + (places - fixed + turn * (used - fixed)) % max(1, count - fixed)
        return jnp.zeros((count,), jnp.int32).at[sequence[jnp.where(places < fixed, places, passed)]].set(jnp.asarray(sizes, jnp.int32))

    sizes = jnp.where(number % 4 == 0, named(crowded, number // 4), named(usual, number - number // 4 - 1))
    mixed = jax.random.permutation(jax.random.fold_in(own, 3), count)
    giver, receiver = mixed[0:count // 2 * 2:2], mixed[1:count // 2 * 2:2]
    room = jnp.minimum(sizes[giver] - 1, bound - sizes[receiver]) // 2
    room = jnp.where((giver == sequence[0]) | (receiver == sequence[0]) | (sizes[receiver] == 0), 0, jnp.maximum(room, 0))
    passed = jax.random.randint(jax.random.fold_in(own, 4), (count // 2,), 0, 1 << 20) % (room + 1)
    sizes = sizes.at[giver].add(-passed).at[receiver].add(passed)
    items = jnp.searchsorted(jnp.cumsum(sizes), jnp.arange(rows * top), side="right").astype(jnp.int32)
    grid = items.reshape(top, rows).T
    grid = grid[jax.random.permutation(jax.random.fold_in(own, 1), rows)]
    turn = jax.random.randint(jax.random.fold_in(own, 2), (rows, 1), 0, top)
    return jnp.take_along_axis(grid, (jnp.arange(top)[None, :] + turn) % top, axis=1)


def shares(amount, total, most, skew, full):
    loads = [(1 << 20) // math.isqrt(rank ** skew) + 1 for rank in range(1, amount + 1)]
    largest = most if full else min(most, max(-(-total // amount), total * loads[0] // sum(loads)))
    least = 1 if total - largest >= amount - 1 else 0
    given, rest = [largest] + [least] * (amount - 1), total - largest - least * (amount - 1)
    while rest > 0:
        movable = [i for i in range(1, amount) if given[i] < largest] or [i for i in range(1, amount) if given[i] < most]
        pool, left = sum([loads[i] for i in movable]), rest
        for i in movable:
            more = min(most - given[i], max(1, left * loads[i] // pool), rest)
            given[i] = given[i] + more
            rest = rest - more
    return np.array(given)


def normal_values(own_key, extent, spread, bound, split=(), kind=jnp.bfloat16):
    values = jax.random.normal(own_key, extent, jnp.float32) * spread
    if len(split) > 0:
        values = block_levels(own_key, extent, split, -0.22, 0.18) * values
    return jnp.clip(values, min=-bound, max=bound).astype(kind)


def setup_inputs(seed: int = 0) -> dict:
    seeds = jax.random.split(jax.random.key(seed), 16)
    hidden_in = normal_values(seeds[0], (TOKENS, D), 1.0, 6.0, ((0, 256),))
    query = draw_query(jax.random.fold_in(seeds[15], 71), 0)
    prefix_pool = draw_prefix_pool(jax.random.fold_in(seeds[15], 71), 0)
    suffix_cache = draw_suffix_cache(jax.random.fold_in(seeds[15], 71), 0)
    block_list = draw_block_list(jax.random.fold_in(seeds[15], 71), 0)
    prefix_count = with_ends(jax.random.randint(seeds[5], (TOKENS,), 1, NB + 1), jax.random.fold_in(seeds[5], 1), 1, NB).astype(jnp.int32)
    suffix_count = with_ends(jax.random.randint(seeds[6], (TOKENS,), 1, SUFFIX + 1), jax.random.fold_in(seeds[6], 1), 1, SUFFIX).astype(jnp.int32)
    value_up = normal_values(seeds[7], (HEADS, LAT, VH), LAT ** -0.5, 0.25, ((0, 32),))
    out_proj = normal_values(seeds[8], (HEADS * VH, D), VH ** -0.5, 0.5, ((0, 32),))
    norm_gain = jnp.clip(1.0 + 0.1 * jax.random.normal(seeds[9], (D,), jnp.float32), 0.5, 1.5).astype(jnp.bfloat16)
    expert_ids_keys = jax.random.split(jax.random.fold_in(seeds[10], 1), TOKENS // REQ_DEV)
    expert_ids_turns = jax.random.permutation(jax.random.fold_in(seeds[10], 3), TOKENS // REQ_DEV)
    expert_ids = jax.vmap(lambda own, number: routed_block(jax.random.fold_in(seeds[10], 2), own, number, REQ_DEV, EXPERTS, TOPK, CAP, 2))(expert_ids_keys, expert_ids_turns).reshape((TOKENS, TOPK))
    gate_weights = jnp.clip(jnp.exp(math.log(1.0) - 2.9996462 * jax.random.uniform(seeds[11], (TOKENS, TOPK), jnp.float32) ** block_levels(seeds[11], (TOKENS, TOPK), ((0, 256),), -0.2, 0.2)), 0.049804688, 1.0).astype(jnp.bfloat16)
    gate_proj = normal_values(seeds[12], (EXPERTS, D, FF), D ** -0.5, 0.078125, ((0, 32), (2, 8)))
    up_proj = normal_values(seeds[13], (EXPERTS, D, FF), D ** -0.5, 0.078125, ((0, 32), (2, 8)))
    down_proj = normal_values(seeds[14], (EXPERTS, FF, D), FF ** -0.5, 0.15625, ((0, 32), (1, 8)))
    return dict(hidden_in=hidden_in, query=query, prefix_pool=prefix_pool, suffix_cache=suffix_cache, block_list=block_list, prefix_count=prefix_count, suffix_count=suffix_count, value_up=value_up, out_proj=out_proj, norm_gain=norm_gain, expert_ids=expert_ids, gate_weights=gate_weights, gate_proj=gate_proj, up_proj=up_proj, down_proj=down_proj)


NEG_FILL = -1e+30
SCORE_SCALE = 192.0 ** (-0.5)
NORM_EPS = 1e-06

def slot_table(expert_rows, expert_total):
    matches = (expert_rows[..., None] == jnp.arange(expert_total, dtype=jnp.int32)).astype(jnp.int32)
    row_load = lax.optimization_barrier(jnp.sum(matches, axis=-2))
    earlier = jnp.cumsum(row_load, axis=-2) - row_load
    return lax.optimization_barrier(jnp.sum(matches * earlier[..., None, :], axis=-1))

def reference(hidden_in, query, prefix_pool, suffix_cache, block_list, prefix_count, suffix_count, value_up, out_proj, norm_gain, expert_ids, gate_weights, gate_proj, up_proj, down_proj):
    groups = TOKENS // REQ_DEV
    pool_rows = prefix_pool.reshape(NBLK, BLOCK, KDIM)
    grouped = (query.reshape(groups, REQ_DEV, HEADS, KDIM), suffix_cache.reshape(groups, REQ_DEV, SUFFIX, KDIM), block_list.reshape(groups, REQ_DEV, NB), prefix_count.reshape(groups, REQ_DEV), suffix_count.reshape(groups, REQ_DEV))

    def attend(member):
        queries, own_keys, block_rows, counts, own_counts = member
        prefix_keys = pool_rows[block_rows].reshape(REQ_DEV, NB * BLOCK, KDIM)
        all_keys = jnp.concatenate([prefix_keys, own_keys], axis=1).astype(jnp.float32)
        prefix_live = (jnp.arange(NB * BLOCK, dtype=jnp.int32) // BLOCK)[None, :] < counts[:, None]
        own_live = jnp.arange(SUFFIX, dtype=jnp.int32)[None, :] < own_counts[:, None]
        live_mask = jnp.concatenate([prefix_live, own_live], axis=1)[:, None, :]
        scores = jnp.einsum('rhk,rnk->rhn', queries.astype(jnp.float32), all_keys) * SCORE_SCALE
        scores = jnp.where(live_mask, scores, NEG_FILL)
        row_max = lax.optimization_barrier(jnp.max(scores, axis=-1, keepdims=True))
        weights = jnp.where(live_mask, jnp.exp(scores - row_max), 0.0)
        denominator = lax.optimization_barrier(jnp.sum(weights, axis=-1))
        rounded = lax.optimization_barrier(weights.astype(jnp.bfloat16)).astype(jnp.float32)
        numerator = jnp.einsum('rhn,rnl->rhl', rounded, all_keys[:, :, :LAT])
        return (numerator / denominator[..., None]).astype(jnp.bfloat16)
    context = lax.map(attend, grouped).reshape(TOKENS, HEADS, LAT)
    head_values = jnp.einsum('thl,hlv->thv', context.astype(jnp.float32), value_up.astype(jnp.float32)).astype(jnp.bfloat16)
    attended = jnp.dot(head_values.reshape(TOKENS, HEADS * VH), out_proj, preferred_element_type=jnp.float32)
    residual_out = hidden_in.astype(jnp.float32) + attended
    widened = residual_out
    scale_rows = lax.rsqrt(lax.optimization_barrier(jnp.mean(widened * widened, axis=-1, keepdims=True)) + NORM_EPS)
    normed = (widened * scale_rows * norm_gain.astype(jnp.float32)).astype(jnp.bfloat16)
    routed = expert_ids.reshape(groups, REQ_DEV, TOPK)
    slots = slot_table(routed, EXPERTS)
    token_rows = normed.reshape(groups, REQ_DEV, D).astype(jnp.float32)
    gates = gate_weights.reshape(groups, REQ_DEV, TOPK).astype(jnp.float32)
    slot_match = slots[..., None] == jnp.arange(CAP, dtype=jnp.int32)

    def per_expert(running, weights_of):
        gate_w, up_w, down_w, expert_index = weights_of
        chosen = (routed == expert_index)[..., None] & slot_match
        select = jnp.any(chosen, axis=2).astype(jnp.float32)
        combine = lax.optimization_barrier(jnp.sum(jnp.where(chosen, gates[..., None], 0.0), axis=2))
        rows_in = jnp.einsum('dtc,dtm->dcm', select, token_rows).astype(jnp.bfloat16).reshape(groups * CAP, D)
        gate_part = jnp.dot(rows_in, gate_w, preferred_element_type=jnp.float32)
        up_part = jnp.dot(rows_in, up_w, preferred_element_type=jnp.float32)
        hidden = (jax.nn.silu(gate_part) * up_part).astype(jnp.bfloat16)
        pieces = jnp.einsum('mgk,gkd->mgd', hidden.reshape(groups * CAP, N_DP, FF_GROUP).astype(jnp.float32), down_w.reshape(N_DP, FF_GROUP, D).astype(jnp.float32))
        pieces = lax.optimization_barrier(pieces.astype(jnp.bfloat16)).astype(jnp.float32)
        outputs = lax.optimization_barrier(jnp.sum(pieces, axis=1)).reshape(groups, CAP, D)
        return (running + jnp.einsum('dtc,dcm->dtm', combine, outputs), None)
    initial = jnp.zeros((groups, REQ_DEV, D), jnp.float32)
    moe_sum, unused = lax.scan(per_expert, initial, (gate_proj, up_proj, down_proj, jnp.arange(EXPERTS, dtype=jnp.int32)))
    return (residual_out, moe_sum.reshape(TOKENS, D))
```

```python
import functools
import jax
import jax.numpy as jnp
from jax import lax
from jax.experimental import pallas as pl
from jax.experimental.pallas import tpu as pltpu
from jax.sharding import PartitionSpec as P

HEADS = 64
LAT = 512
BLOCK = 64
SUFFIX = 128
KDIM = 576
KPAD = 640
D = 5120
HALF = 2560
FFG = 192
TABLE = 128

NEG_FILL = -1e30
SCORE_SCALE = 192.0 ** (-0.5)
NORM_EPS = 1e-06

NX, NY, NZ = 4, 4, 8
MESH = pl.DeviceIdType.MESH
F32 = jnp.float32
BF16 = jnp.bfloat16


def here():
    z = lax.axis_index("dp")
    e = lax.axis_index("expert")
    core = lax.rem(e, 2)
    chip = lax.div(e, 2)
    return z, lax.div(chip, NX), lax.rem(chip, NX), core


def dev(z, y, x, core):
    return (z, (y * NX + x) * 2 + core)


def step(v, by, n):
    return lax.rem(v + by + n, n)


def greet(peers):
    barrier = pltpu.get_barrier_semaphore()
    for peer in peers:
        pl.semaphore_signal(barrier, inc=1, device_id=peer, device_id_type=MESH)
    pl.semaphore_wait(barrier, len(peers))


def torus_peers(z, y, x, c):
    peers = [dev(step(z, j, NZ), y, x, c) for j in range(1, NZ)]
    peers += [dev(z, y, step(x, s, NX), c) for s in (1, -1)]
    peers += [dev(z, step(y, s, NY), x, c) for s in (1, -1)]
    return peers + [dev(z, y, x, 1 - c)]


class Post:
    def __init__(self, send, recv):
        self.send, self.recv, self.count, self.sent = send, recv, 0, []

    def put(self, src, dst, to, lands):
        i = self.count
        self.count += 1
        copy = pltpu.make_async_remote_copy(
            src_ref=src, dst_ref=dst, send_sem=self.send.at[i], recv_sem=self.recv.at[i],
            device_id=to, device_id_type=MESH,
        )
        copy.start()
        self.sent.append(copy)
        return pltpu.make_async_remote_copy(
            src_ref=lands, dst_ref=lands, send_sem=self.send.at[i], recv_sem=self.recv.at[i],
            device_id=to, device_id_type=MESH,
        ).wait_recv

    def drain(self):
        for copy in self.sent:
            copy.wait_send()


def gather(post, block, g, rows, local_sem):
    z, y, x, c = here()
    xp, xm, x2 = step(x, 1, NX), step(x, -1, NX), step(x, 2, NX)
    yp, ym, y2 = step(y, 1, NY), step(y, -1, NY), step(y, 2, NY)
    quarter = 2 * rows
    a_lo, a_hi, a_all = pl.ds(0, quarter), pl.ds(quarter, quarter), pl.ds(0, 2 * quarter)
    b_lo, b_hi, b_all = (
        pl.ds(2 * quarter, quarter), pl.ds(3 * quarter, quarter), pl.ds(2 * quarter, 2 * quarter)
    )

    def zrows(at):
        return pl.ds(pl.multiple_of(at * rows, rows), rows)

    def slot(yy, xx, part):
        return g.at[c, yy, xx, part]

    keep = pltpu.make_async_copy(block, slot(y, x, zrows(z)), local_sem)
    keep.start()
    arrive = [
        post.put(block, slot(y, x, zrows(z)), dev(step(z, j, NZ), y, x, c), slot(y, x, zrows(step(z, -j, NZ))))
        for j in range(1, NZ)
    ]
    yield []
    keep.wait()
    for wait in arrive:
        wait()

    from_sibling = {}

    def sibling(name, yy, xx, part):
        from_sibling[name] = post.put(
            slot(yy, xx, part), slot(yy, xx, part), dev(z, y, x, 1 - c), g.at[1 - c, yy, xx, part]
        )

    def along_x(yy, xx, part, by):
        return post.put(
            slot(yy, xx, part), slot(yy, xx, part), dev(z, y, step(x, by, NX), c),
            slot(yy, step(xx, -by, NX), part),
        )

    def along_y(yy, xx, part, by):
        return post.put(
            slot(yy, xx, part), slot(yy, xx, part), dev(z, step(y, by, NY), x, c),
            slot(step(yy, -by, NY), xx, part),
        )

    a1p, a1m = along_x(y, x, a_all, 1), along_x(y, x, a_all, -1)
    b1p, b1m = along_y(y, x, b_all, 1), along_y(y, x, b_all, -1)
    sibling(("a", 0, 0), y, x, a_all)
    sibling(("b", 0, 0), y, x, b_all)
    xs, ys = {0: x, -1: xm, 1: xp, 2: x2}, {0: y, -1: ym, 1: yp, 2: y2}
    a2, b2 = {}, {}

    def second_a(o):
        a2[o] = (along_y(y, xs[o], a_all, 1), along_y(y, xs[o], a_all, -1))

    def second_b(o):
        b2[o] = (along_x(ys[o], x, b_all, 1), along_x(ys[o], x, b_all, -1))

    second_a(0)
    second_b(0)
    a1p()
    fa_lo = along_x(y, xm, a_lo, 1)
    b1p()
    fb_lo = along_y(ym, x, b_lo, 1)
    a1m()
    fa_hi = along_x(y, xp, a_hi, -1)
    b1m()
    fb_hi = along_y(yp, x, b_hi, -1)
    for o in (-1, 1):
        second_a(o)
        second_b(o)
        sibling(("a", 0, o), y, xs[o], a_all)
        sibling(("b", o, 0), ys[o], x, b_all)

    def done(*chunks):
        for dy, dx in chunks:
            from_sibling[("a", dy, dx)]()
            from_sibling[("b", dy, dx)]()
        return [(ys[dy], xs[dx]) for dy, dx in chunks]

    yield done((0, 0))
    fa_lo()
    fa_hi()
    second_a(2)
    fb_lo()
    fb_hi()
    second_b(2)
    sibling(("a", 0, 2), y, x2, a_all)
    sibling(("b", 2, 0), y2, x, b_all)
    last_a, last_b = {}, {}
    ready = {
        0: [(-1, 0), (1, 0), (0, -1), (0, 1)], -1: [(-1, -1)], 1: [(1, 1), (1, -1), (-1, 1)], 2: [],
    }
    late = []
    for o in (0, -1, 1, 2):
        a2[o][0]()
        lo_a = along_y(ym, xs[o], a_lo, 1)
        b2[o][0]()
        lo_b = along_x(ys[o], xm, b_lo, 1)
        a2[o][1]()
        last_a[o] = (lo_a, along_y(yp, xs[o], a_hi, -1))
        b2[o][1]()
        last_b[o] = (lo_b, along_x(ys[o], xp, b_hi, -1))
        for s in (-1, 1):
            sibling(("a", s, o), ys[s], xs[o], a_all)
            sibling(("b", o, s), ys[o], xs[s], b_all)
        for chunk in late:
            yield done(chunk)
        late = ready[o]
    for chunk in late:
        yield done(chunk)
    late = []
    for o in (0, -1, 1, 2):
        for wait in last_a[o] + last_b[o]:
            wait()
        sibling(("a", 2, o), y2, xs[o], a_all)
        sibling(("b", o, 2), ys[o], x2, b_all)
        for chunk in late:
            yield done(chunk)
        late = [(2, o), (o, 2)] if o != 2 else [(2, 2)]
    for chunk in late:
        yield done(chunk)


GATHER_COPIES = 96


def attend_kernel(q_ref, own_ref, block_ref, bias_ref, out_ref, g, top, total, acc, send, recv, local_sem):
    post = Post(send, recv)
    greet(torus_peers(*here()))

    def merge(keys, bias, first=False):
        q = q_ref[...]
        scores = jnp.concatenate(
            [lax.dot_general(q, k, (((1,), (1,)), ((), ())), preferred_element_type=F32) for k in keys], axis=1
        )
        rows, width = scores.shape
        scores = (scores.reshape(rows // 8, 8, width) * SCORE_SCALE + bias[None]).reshape(rows, width)
        best = jnp.max(scores, axis=1, keepdims=True)
        if not first:
            best = jnp.maximum(best, top[...])
        weights = jnp.exp(scores - best)
        summed = jnp.sum(weights, axis=1, keepdims=True)
        weights = weights.astype(BF16)
        each = width // len(keys)
        mixed = sum(
            jnp.dot(weights[:, i * each : (i + 1) * each], k[:, :LAT], preferred_element_type=F32)
            for i, k in enumerate(keys)
        )
        if first:
            total[...] = summed
            acc[...] = mixed
        else:
            scale = jnp.exp(top[...] - best)
            total[...] = total[...] * scale + summed
            acc[...] = acc[...] * scale + mixed
        top[...] = best

    started = False
    for chunks in gather(post, block_ref, g, 32, local_sem):
        if not started:
            merge([own_ref[...]], bias_ref[16], first=True)
            started = True
        for yy, xx in chunks:
            merge([g[0, yy, xx], g[1, yy, xx]], bias_ref[yy * NX + xx])
    out_ref[...] = (acc[...] / total[...]).astype(BF16)
    post.drain()


def attend(q, own, block, bias):
    rows = q.shape[0]
    return pl.pallas_call(
        attend_kernel,
        out_shape=jax.ShapeDtypeStruct((rows, LAT), BF16),
        in_specs=[pl.BlockSpec(memory_space=pltpu.VMEM)] * 4,
        out_specs=pl.BlockSpec(memory_space=pltpu.VMEM),
        scratch_shapes=[
            pltpu.VMEM((2, NY, NX, NZ * 32, KPAD), BF16),
            pltpu.VMEM((rows, 1), F32),
            pltpu.VMEM((rows, 1), F32),
            pltpu.VMEM((rows, LAT), F32),
            pltpu.SemaphoreType.DMA((GATHER_COPIES,)),
            pltpu.SemaphoreType.DMA((GATHER_COPIES,)),
            pltpu.SemaphoreType.DMA,
        ],
        compiler_params=pltpu.CompilerParams(
            collective_id=0, has_side_effects=True, vmem_limit_bytes=56 * 2**20
        ),
        name="attend",
    )(q, own, block, bias)


def project_kernel(
    ctx_ref, up_ref, proj_hbm, hidden_ref, gain_ref, res_ref, norm_ref,
    ctx_in, proj, other, from_other, parts, parts_in, full,
    local_sem, ctx_send, ctx_recv, send, recv, sib_send, sib_recv,
):
    z, y, x, c = here()
    e = (y * NX + x) * 2 + c
    chip = y * NX + x
    devices = 2 * NX * NY
    chips = NX * NY

    loads = [
        pltpu.make_async_copy(
            proj_hbm.at[:, pl.ds(pl.multiple_of(half * HALF, 128), HALF)], proj.at[i], local_sem.at[i]
        )
        for i, half in enumerate((c, 1 - c))
    ]
    for load in loads:
        load.start()
    barrier = pltpu.get_barrier_semaphore()

    def hello(j, carry):
        pl.semaphore_signal(
            barrier, inc=1, device_id=(z, lax.rem(e + j, devices)), device_id_type=MESH
        )
        return carry

    lax.fori_loop(1, devices, hello, 0)
    pl.semaphore_wait(barrier, devices - 1)

    def ctx_copy(j):
        to = lax.rem(e + j, devices)
        return pltpu.make_async_remote_copy(
            src_ref=ctx_ref.at[to], dst_ref=ctx_in.at[e], send_sem=ctx_send.at[j], recv_sem=ctx_recv.at[j],
            device_id=(z, to), device_id_type=MESH,
        )

    def ctx_arrival(j):
        source = lax.rem(e - j + devices, devices)
        return pltpu.make_async_remote_copy(
            src_ref=ctx_in.at[source], dst_ref=ctx_in.at[source], send_sem=ctx_send.at[j],
            recv_sem=ctx_recv.at[j], device_id=(z, source), device_id_type=MESH,
        )

    def each(low, high, act):
        def body(j, carry):
            act(j)
            return carry

        lax.fori_loop(low, high, body, 0)

    each(1, devices, lambda j: ctx_copy(j).start())
    mine = pltpu.make_async_copy(ctx_ref.at[e], ctx_in.at[e], local_sem.at[2])
    mine.start()
    mine.wait()
    for load in loads:
        load.wait()
    each(1, devices, lambda j: ctx_arrival(j).wait_recv())

    context = ctx_in[...].reshape(devices * 8, LAT)
    first = jnp.dot(context, up_ref[0], preferred_element_type=F32).reshape(chips, 16, 128)
    second = jnp.dot(context, up_ref[1], preferred_element_type=F32).reshape(chips, 16, 128)
    upper = lax.broadcasted_iota(jnp.int32, (chips, 8, 128), 1) < 4

    def swap(v):
        return jnp.concatenate([v[:, 4:], v[:, :4]], axis=1)

    left = jnp.where(upper, first[:, :8], swap(first[:, 8:]))
    right = jnp.where(upper, swap(second[:, :8]), second[:, 8:])
    values = jnp.concatenate([left, right], axis=2).reshape(chips * 8, 256).astype(BF16)

    tile = 640
    for i in range(HALF // tile):
        columns = pl.ds(i * tile, tile)
        part = jnp.dot(values, proj[1, :, columns], preferred_element_type=F32)
        other[:, :, columns] = part.reshape(chips, 8, tile).astype(BF16)
    other[chip] = (other[chip].astype(F32) + hidden_ref[1]).astype(BF16)
    sib = pltpu.make_async_remote_copy(
        src_ref=other, dst_ref=from_other, send_sem=sib_send.at[0], recv_sem=sib_recv.at[0],
        device_id=dev(z, y, x, 1 - c), device_id_type=MESH,
    )
    sib.start()
    for i in range(HALF // tile):
        columns = pl.ds(i * tile, tile)
        part = jnp.dot(values, proj[0, :, columns], preferred_element_type=F32)
        full[:, :, columns] = part.reshape(chips, 8, tile)
    sib.wait()

    def total(j, carry):
        full[j] = full[j] + from_other[j].astype(F32)
        parts[j] = full[j].astype(BF16)
        return carry

    lax.fori_loop(0, chips, total, 0)

    def part_copy(j):
        to = lax.rem(chip + j, chips)
        return pltpu.make_async_remote_copy(
            src_ref=parts.at[to], dst_ref=parts_in.at[j], send_sem=send.at[j], recv_sem=recv.at[j],
            device_id=(z, to * 2 + c), device_id_type=MESH,
        )

    each(1, chips, lambda j: part_copy(j).start())
    res_ref[c] = full[chip] + hidden_ref[0]
    each(1, chips, lambda j: part_copy(j).wait_recv())

    def gathered(j, carry):
        return carry + parts_in[j].astype(F32)

    res_ref[c] = lax.fori_loop(1, chips, gathered, res_ref[c])
    swap_copy = pltpu.make_async_remote_copy(
        src_ref=res_ref.at[c], dst_ref=res_ref.at[c], send_sem=sib_send.at[1], recv_sem=sib_recv.at[1],
        device_id=dev(z, y, x, 1 - c), device_id_type=MESH,
    )
    swap_copy.start()
    swap_in = pltpu.make_async_remote_copy(
        src_ref=res_ref.at[1 - c], dst_ref=res_ref.at[1 - c], send_sem=sib_send.at[1],
        recv_sem=sib_recv.at[1], device_id=dev(z, y, x, 1 - c), device_id_type=MESH,
    )
    swap_in.wait_recv()
    squares = sum(jnp.sum(res_ref[h] * res_ref[h], axis=1, keepdims=True) for h in range(2))
    scale = lax.rsqrt(squares * (1.0 / D) + NORM_EPS)
    norm_ref[...] = (res_ref[c] * scale * gain_ref[c]).astype(BF16)
    swap_copy.wait_send()
    each(1, devices, lambda j: ctx_copy(j).wait_send())
    each(1, chips, lambda j: part_copy(j).wait_send())


def project(ctx, value_up, out_proj, hidden, gain):
    chips = NX * NY
    vmem = pl.BlockSpec(memory_space=pltpu.VMEM)
    return pl.pallas_call(
        project_kernel,
        out_shape=(
            jax.ShapeDtypeStruct((2, 8, HALF), F32),
            jax.ShapeDtypeStruct((8, HALF), BF16),
        ),
        in_specs=[vmem, vmem, pl.BlockSpec(memory_space=pl.ANY), vmem, vmem],
        out_specs=(vmem, vmem),
        scratch_shapes=[
            pltpu.VMEM((2 * chips, 8, LAT), BF16),
            pltpu.VMEM((2, 256, HALF), BF16),
            pltpu.VMEM((chips, 8, HALF), BF16),
            pltpu.VMEM((chips, 8, HALF), BF16),
            pltpu.VMEM((chips, 8, HALF), BF16),
            pltpu.VMEM((chips, 8, HALF), BF16),
            pltpu.VMEM((chips, 8, HALF), F32),
            pltpu.SemaphoreType.DMA((3,)),
            pltpu.SemaphoreType.DMA((2 * chips,)),
            pltpu.SemaphoreType.DMA((2 * chips,)),
            pltpu.SemaphoreType.DMA((chips,)),
            pltpu.SemaphoreType.DMA((chips,)),
            pltpu.SemaphoreType.DMA((2,)),
            pltpu.SemaphoreType.DMA((2,)),
        ],
        compiler_params=pltpu.CompilerParams(
            collective_id=1, has_side_effects=True, vmem_limit_bytes=56 * 2**20
        ),
        name="project",
    )(ctx, value_up, out_proj, hidden, gain)


def ring_sum(post, block, into, pos, n, lo, hi, to):
    plus, minus, far = step(pos, 1, n), step(pos, -1, n), step(pos, 2, n)
    up, down = to(1), to(-1)

    def put(src, i, device):
        return post.put(src, into.at[i], device, into.at[i])

    far_up = put(block(far, lo), 0, up)
    far_down = put(block(far, hi), 1, down)
    free_up = put(block(plus, hi), 2, up)
    free_down = put(block(minus, lo), 3, down)
    yield
    far_up()
    add(block(plus, lo), into.at[0])
    last_up = put(block(plus, lo), 4, up)
    far_down()
    add(block(minus, hi), into.at[1])
    last_down = put(block(minus, hi), 5, down)
    yield
    free_up()
    last_down()
    add(block(pos, hi), into.at[2], into.at[5])
    free_down()
    last_up()
    add(block(pos, lo), into.at[3], into.at[4])


def add(ref, *others):
    if len(ref.shape) == 3:
        for i in range(ref.shape[0]):
            add(ref.at[i], *[o.at[i] for o in others])
        return
    value = ref[...].astype(F32)
    for o in others:
        value = value + o[...].astype(F32)
    ref[...] = value.astype(BF16)


MOE_COPIES = 144


def moe_kernel(
    norm_ref, table_ref, gate_hbm, up_hbm, down_hbm, out_ref,
    block, g, gate, up, down, hidden, other, from_other, sums, ring_a, ring_b, ring_c, ring_d, z_in, final,
    send, recv, local_sem,
):
    z, y, x, c = here()
    loads = [
        pltpu.make_async_copy(gate_hbm.at[0], gate, local_sem.at[1]),
        pltpu.make_async_copy(up_hbm.at[0], up, local_sem.at[2]),
    ] + [
        pltpu.make_async_copy(
            down_hbm.at[0, :, pl.ds(pl.multiple_of(half * HALF, 128), HALF)], down.at[i], local_sem.at[3 + i]
        )
        for i, half in enumerate((c, 1 - c))
    ]
    for load in loads:
        load.start()
    post = Post(send, recv)
    greet(torus_peers(z, y, x, c))
    block[:, :HALF] = norm_ref[...]
    block[:, HALF:] = table_ref[...]
    for _ in gather(post, block, g, 8, local_sem.at[0]):
        pass
    for load in loads:
        load.wait()

    e = (y * NX + x) * 2 + c
    ours = (lax.broadcasted_iota(jnp.int32, (256, TABLE), 1) == e).astype(F32)

    def hidden_rows(i, carry):
        rows = [g[h, i].reshape(256, HALF + TABLE) for h in range(2)]
        weight = jnp.sum(
            (rows[0][:, HALF:].astype(F32) + rows[1][:, HALF:].astype(F32)) * ours, axis=1, keepdims=True
        )

        def product(w):
            return jnp.dot(rows[0][:, :HALF], w[:HALF], preferred_element_type=F32) + jnp.dot(
                rows[1][:, :HALF], w[HALF:], preferred_element_type=F32
            )

        gated = product(gate)
        raised = product(up)
        hidden[i] = (gated / (1.0 + jnp.exp(-gated)) * raised * weight).astype(BF16)
        return carry

    lax.fori_loop(0, NY, hidden_rows, 0)

    xs = [step(x, o, NX) for o in range(NX)]
    ys = [step(y, o, NY) for o in range(NY)]
    tile = 640
    order = (ys[2], ys[1], ys[3], ys[0])
    waits = []
    for yy in order:
        rows = hidden[yy]
        for i in range(HALF // tile):
            columns = pl.ds(i * tile, tile)
            part = jnp.dot(rows, down[1, :, columns], preferred_element_type=F32)
            other[yy, :, :, columns] = part.reshape(NX, 64, tile).astype(BF16)
        waits.append(post.put(other.at[yy], from_other.at[yy], dev(z, y, x, 1 - c), from_other.at[yy]))
    for yy, wait in zip(order, waits):
        wait()
        rows = hidden[yy]
        for i in range(HALF // tile):
            columns = pl.ds(i * tile, tile)
            part = jnp.dot(rows, down[0, :, columns], preferred_element_type=F32).reshape(NX, 64, tile)
            sums[yy, :, :, columns] = (part + from_other[yy, :, :, columns].astype(F32)).astype(BF16)

    a_lo, a_hi, b_lo, b_hi = [pl.ds(16 * i, 16) for i in range(4)]

    def to_x(s):
        return dev(z, y, step(x, s, NX), c)

    def to_y(s):
        return dev(z, step(y, s, NY), x, c)

    def together(*rings):
        for _ in zip(*rings):
            pass
        for ring in rings:
            for _ in ring:
                pass

    together(
        ring_sum(post, lambda p, r: sums.at[p, :, r], ring_a, y, NY, a_lo, a_hi, to_y),
        ring_sum(post, lambda p, r: sums.at[:, p, r], ring_b, x, NX, b_lo, b_hi, to_x),
    )
    together(
        ring_sum(post, lambda p, r: sums.at[y, p, r], ring_c, x, NX, a_lo, a_hi, to_x),
        ring_sum(post, lambda p, r: sums.at[p, x, r], ring_d, y, NY, b_lo, b_hi, to_y),
    )

    def zrows(at):
        return pl.ds(pl.multiple_of(at * 8, 8), 8)

    waits = [
        post.put(sums.at[y, x, zrows(step(z, j, NZ))], z_in.at[j], dev(step(z, j, NZ), y, x, c), z_in.at[j])
        for j in range(1, NZ)
    ]
    keep = pltpu.make_async_copy(sums.at[y, x, zrows(z)], z_in.at[0], local_sem.at[0])
    keep.start()
    keep.wait()
    for wait in waits:
        wait()
    value = z_in[0].astype(F32)
    for j in range(1, NZ):
        value = value + z_in[j].astype(F32)
    final[c] = value
    post.put(final.at[c], final.at[c], dev(z, y, x, 1 - c), final.at[1 - c])()
    upper = lax.broadcasted_iota(jnp.int32, (4, HALF), 0) * 0 + c == 0
    for h in range(2):
        out_ref[:, h * HALF : (h + 1) * HALF] = jnp.where(upper, final[h, :4], final[h, 4:])
    post.drain()


def moe(normed, table, gate_proj, up_proj, down_proj):
    vmem = pl.BlockSpec(memory_space=pltpu.VMEM)
    hbm = pl.BlockSpec(memory_space=pl.ANY)
    return pl.pallas_call(
        moe_kernel,
        out_shape=jax.ShapeDtypeStruct((4, D), F32),
        in_specs=[vmem, vmem, hbm, hbm, hbm],
        out_specs=vmem,
        scratch_shapes=[
            pltpu.VMEM((8, HALF + TABLE), BF16),
            pltpu.VMEM((2, NY, NX, NZ * 8, HALF + TABLE), BF16),
            pltpu.VMEM((D, FFG), BF16),
            pltpu.VMEM((D, FFG), BF16),
            pltpu.VMEM((2, FFG, HALF), BF16),
            pltpu.VMEM((NY, 256, FFG), BF16),
            pltpu.VMEM((NY, NX, 64, HALF), BF16),
            pltpu.VMEM((NY, NX, 64, HALF), BF16),
            pltpu.VMEM((NY, NX, 64, HALF), BF16),
            pltpu.VMEM((6, NX, 16, HALF), BF16),
            pltpu.VMEM((6, NY, 16, HALF), BF16),
            pltpu.VMEM((6, 16, HALF), BF16),
            pltpu.VMEM((6, 16, HALF), BF16),
            pltpu.VMEM((NZ, 8, HALF), BF16),
            pltpu.VMEM((2, 8, HALF), F32),
            pltpu.SemaphoreType.DMA((MOE_COPIES,)),
            pltpu.SemaphoreType.DMA((MOE_COPIES,)),
            pltpu.SemaphoreType.DMA((5,)),
        ],
        compiler_params=pltpu.CompilerParams(
            collective_id=2, has_side_effects=True, vmem_limit_bytes=56 * 2**20
        ),
        name="moe",
    )(normed, table, gate_proj, up_proj, down_proj)


def per_device(
    hidden_in, query, prefix_pool, suffix_cache, block_list, prefix_count, suffix_count, value_up,
    out_proj, norm_gain, expert_ids, gate_weights, gate_proj, up_proj, down_proj,
):
    e = lax.axis_index("expert")
    core, chip = lax.rem(e, 2), lax.div(e, 2)

    half = BLOCK // 2 * KDIM
    block = lax.dynamic_slice(prefix_pool, (chip, core * half), (1, half)).reshape(BLOCK // 2, KDIM)
    block = jnp.pad(block, ((0, 0), (0, KPAD - KDIM)))
    q = query.reshape(4, 32, 2, KDIM).transpose(1, 2, 0, 3).reshape(256, KDIM)
    q = jnp.pad(q, ((0, 0), (0, KPAD - KDIM)))
    own = jnp.pad(suffix_cache.reshape(4 * SUFFIX, KDIM), ((0, 0), (0, KPAD - KDIM)))
    in_prefix = jnp.arange(32, dtype=jnp.int32)[None, :] < prefix_count[:, None]
    listed = jnp.where(in_prefix, block_list, -1)
    member = jnp.any(listed[:, :, None] == jnp.arange(128, dtype=jnp.int32), axis=1)
    member = member.reshape(4, NZ, 16).transpose(2, 0, 1)
    pool_live = jnp.broadcast_to(member[:, None, :, None, :, None], (16, 2, 4, 2, NZ, 32)).reshape(16, 8, 512)
    row = jnp.arange(4 * SUFFIX, dtype=jnp.int32)
    own_live = (row // SUFFIX == jnp.arange(4, dtype=jnp.int32)[:, None]) & (
        row % SUFFIX < suffix_count[:, None]
    )
    own_live = jnp.concatenate([own_live, own_live], axis=0)
    bias = jnp.where(jnp.concatenate([pool_live, own_live[None]], axis=0), 0.0, NEG_FILL).astype(F32)
    context = attend(q, own, block, bias)

    mine = (jnp.arange(8, dtype=jnp.int32) // 4 == core)[:, None]
    hidden = jnp.where(mine, jnp.concatenate([hidden_in, hidden_in], axis=0).astype(F32), 0.0)
    hidden = hidden.reshape(8, 2, HALF).transpose(1, 0, 2)
    hidden = jnp.where(core == 0, hidden, hidden[::-1])
    gain = norm_gain.astype(F32).reshape(2, 1, HALF)
    residual, normed = project(context.reshape(32, 8, LAT), value_up, out_proj, hidden, gain)
    residual_out = lax.dynamic_slice(residual, (0, core * 4, 0), (2, 4, HALF)).transpose(1, 0, 2).reshape(4, D)

    named = expert_ids[:, :, None] == jnp.arange(TABLE, dtype=jnp.int32)
    table = jnp.sum(jnp.where(named, gate_weights.astype(F32)[:, :, None], 0.0), axis=1)
    table = jnp.where(mine, jnp.concatenate([table, table], axis=0), 0.0).astype(BF16)
    return residual_out, moe(normed, table, gate_proj, up_proj, down_proj)


def solution(mesh):
    rows = P(("dp", "expert"), None)
    in_specs = (
        rows, rows, P("dp", None), rows, rows, P(("dp", "expert")), P(("dp", "expert")),
        P("expert", None, None), P("expert", None), P(), rows, rows,
        P("expert", None, "dp"), P("expert", None, "dp"), P("expert", "dp", None),
    )
    return jax.shard_map(
        per_device, mesh=mesh, in_specs=in_specs, out_specs=(rows, rows), check_vma=False
    )
```

```python
import functools
import jax
import jax.numpy as jnp
from jax import lax
from jax.experimental import pallas as pl
from jax.experimental.pallas import tpu as pltpu
from jax.sharding import PartitionSpec as P

HEADS = 64
LAT = 512
BLOCK = 64
SUFFIX = 128
KDIM = 576
KPAD = 640
D = 5120
HALF = 2560
FFG = 192
TABLE = 128

NEG_FILL = -1e30
SCORE_SCALE = 192.0 ** (-0.5)
NORM_EPS = 1e-06

NX, NY, NZ = 4, 4, 8
MESH = pl.DeviceIdType.MESH
F32 = jnp.float32
BF16 = jnp.bfloat16


def here():
    z = lax.axis_index("dp")
    e = lax.axis_index("expert")
    core = lax.rem(e, 2)
    chip = lax.div(e, 2)
    return z, lax.div(chip, NX), lax.rem(chip, NX), core


def dev(z, y, x, core):
    return (z, (y * NX + x) * 2 + core)


def step(v, by, n):
    return lax.rem(v + by + n, n)


class Post:
    def __init__(self, send, recv):
        self.send, self.recv, self.count, self.sent = send, recv, 0, []

    def put(self, src, dst, to, lands):
        i = self.count
        self.count += 1
        copy = pltpu.make_async_remote_copy(
            src_ref=src, dst_ref=dst, send_sem=self.send.at[i], recv_sem=self.recv.at[i],
            device_id=to, device_id_type=MESH,
        )
        copy.start()
        self.sent.append(copy)
        return pltpu.make_async_remote_copy(
            src_ref=lands, dst_ref=lands, send_sem=self.send.at[i], recv_sem=self.recv.at[i],
            device_id=to, device_id_type=MESH,
        ).wait_recv

    def drain(self):
        for copy in self.sent:
            copy.wait_send()


def gather(post, block, g, local_sem):
    z, y, x, c = here()
    xs = {o: step(x, o, NX) for o in (0, -1, 1, 2)}
    ys = {o: step(y, o, NY) for o in (0, -1, 1, 2)}
    zs = {o: step(z, o, NZ) for o in range(-4, 5)}
    other = dev(z, y, x, 1 - c)

    def move(view, arriving, to):
        return post.put(view, view, to, arriving)

    block_ab, block_c = block
    whole = g.c_block is None
    keeps = [
        pltpu.make_async_copy(block_ab, g.ab(c, y, x, z, 1), local_sem.at[0]),
        pltpu.make_async_copy(block_c, g.c_slab(c, z) if whole else g.c_block(c, y, x, z), local_sem.at[1]),
    ]
    for keep in keeps:
        keep.start()
    c_x = [] if whole else [
        post.put(block_c, g.c_block(c, y, x, z), dev(z, y, step(x, o, NX), c), g.c_block(c, y, step(x, -o, NX), z))
        for o in (1, 3, 2)
    ]
    ab_z = [
        post.put(block_ab, g.ab(c, y, x, z, 1), dev(step(z, j, NZ), y, x, c), g.ab(c, y, x, step(z, -j, NZ), 1))
        for j in (1, 7, 2, 6, 3, 5, 4)
    ]
    for keep in keeps:
        keep.wait()
    from_sibling = {}

    def sibling_c(dz):
        from_sibling[dz] = move(g.c_slab(c, zs[dz]), g.c_slab(1 - c, zs[dz]), other)

    def along_z(dz, by, part):
        return move(g.c_slab(c, zs[dz], part), g.c_slab(c, zs[dz - by], part), dev(zs[by], y, x, c))

    up, down = {}, {}

    def begin_z():
        for part in range(PARTS):
            up[part], down[PARTS - 1 - part] = along_z(0, 1, part), along_z(0, -1, PARTS - 1 - part)
        sibling_c(0)

    ring_events = [(s, part) for s in (1, 2, 3) for part in range(PARTS)]

    def ring_z(events):
        for _ in range(events):
            s, part = ring_events.pop(0)
            up[part]()
            if s < 3 or part < PARTS // 2:
                up[part] = along_z(-s, 1, part)
            back = PARTS - 1 - part
            down[back]()
            if s < 3 or back >= PARTS // 2:
                down[back] = along_z(s, -1, back)
            if part == PARTS - 1:
                sibling_c(-s)
                sibling_c(s)

    for wait in c_x:
        wait()
    c_y = [] if whole else [
        move(g.c_row(c, y, z), g.c_row(c, step(y, -o, NY), z), dev(z, step(y, o, NY), x, c)) for o in (1, 3, 2)
    ]
    if whole:
        begin_z()
    yield []
    for wait in ab_z:
        wait()

    halves = {"a": (0, 4), "b": (4, 4), "a_lo": (0, 2), "a_hi": (2, 2), "b_lo": (4, 2), "b_hi": (6, 2)}
    def sibling(name, dy, dx):
        yy, xx = ys[dy], xs[dx]
        from_sibling[(name, dy, dx)] = move(g.ab(c, yy, xx, *halves[name]), g.ab(1 - c, yy, xx, *halves[name]), other)

    def along_x(dy, dx, name, by):
        yy, xx = ys[dy], xs[dx]
        return move(
            g.ab(c, yy, xx, *halves[name]), g.ab(c, yy, step(xx, -by, NX), *halves[name]), dev(z, y, xs[by], c)
        )

    def along_y(dy, dx, name, by):
        yy, xx = ys[dy], xs[dx]
        return move(
            g.ab(c, yy, xx, *halves[name]), g.ab(c, step(yy, -by, NY), xx, *halves[name]), dev(z, ys[by], x, c)
        )

    a1p, b1p = along_x(0, 0, "a", 1), along_y(0, 0, "b", 1)
    a1m, b1m = along_x(0, 0, "a", -1), along_y(0, 0, "b", -1)
    sibling("a", 0, 0)
    sibling("b", 0, 0)
    a2, b2 = {}, {}

    def second(o):
        a2[o] = (along_y(0, o, "a", 1), along_y(0, o, "a", -1))
        b2[o] = (along_x(o, 0, "b", 1), along_x(o, 0, "b", -1))

    second(0)
    if not whole:
        for wait in c_y:
            wait()
        begin_z()
    else:
        ring_z(PARTS)
    a1p()
    fa_lo = along_x(0, -1, "a_lo", 1)
    b1p()
    fb_lo = along_y(-1, 0, "b_lo", 1)
    a1m()
    fa_hi = along_x(0, 1, "a_hi", -1)
    b1m()
    fb_hi = along_y(1, 0, "b_hi", -1)
    for o in (-1, 1):
        second(o)
        sibling("a", 0, o)
        sibling("b", o, 0)

    def done(*parts):
        ready = []
        for part in parts:
            if isinstance(part, int):
                from_sibling[part]()
                ready.append((zs[part],))
            else:
                from_sibling[("a",) + part]()
                from_sibling[("b",) + part]()
                ready.append((ys[part[0]], xs[part[1]]))
        return ready

    queue = [(0, 0), 0]

    def some():
        return done(queue.pop(0)) if queue else []

    yield some()
    ring_z(PARTS)
    yield some()
    fa_lo()
    fa_hi()
    fb_lo()
    fb_hi()
    second(2)
    sibling("a", 0, 2)
    sibling("b", 2, 0)

    last_a, last_b = {}, {}
    ready = {
        0: [(-1, 0), (1, 0), (0, -1), (0, 1)], -1: [(-1, -1)], 1: [(1, 1), (1, -1), (-1, 1)], 2: [],
    }
    seen = 0
    for o in (0, -1, 1, 2):
        ring_z(min(PARTS // 2, len(ring_events)))
        yield some()
        a2[o][0]()
        lo_a = along_y(-1, o, "a_lo", 1)
        b2[o][0]()
        lo_b = along_x(o, -1, "b_lo", 1)
        yield some()
        a2[o][1]()
        last_a[o] = (lo_a, along_y(1, o, "a_hi", -1))
        b2[o][1]()
        last_b[o] = (lo_b, along_x(o, 1, "b_hi", -1))
        for side in (-1, 1):
            sibling("a", side, o)
            sibling("b", o, side)
        yield some()
        now = 3 - -(-len(ring_events) // PARTS)
        queue += ready[o] + [d for n in range(seen + 1, now + 1) for d in (-n, n)]
        seen = now
    for o in (0, -1, 1, 2):
        for wait in last_a[o]:
            wait()
        sibling("a", 2, o)
        yield some()
        for wait in last_b[o]:
            wait()
        sibling("b", o, 2)
        yield some()
        queue += [(2, o), (o, 2)] if o != 2 else [(2, 2)]
    for part in range(PARTS // 2):
        up[part]()
        down[PARTS - 1 - part]()
    sibling_c(4)
    queue += [4]
    while queue:
        yield some()


COPIES = 400
PARTS = 4


class Pool:
    AB, C = 24, 128
    c_block = None

    def __init__(self, ab, c):
        self.g_ab, self.g_c = ab, c

    def ab(self, core, yy, xx, z0, nz):
        return self.g_ab.at[core, yy, xx, pl.ds(z0, nz)]

    def c_slab(self, core, zz, part=None):
        if part is None:
            return self.g_c.at[core, zz]
        return self.g_c.at[core, zz, pl.ds(part * (self.C // PARTS), self.C // PARTS)]


class Tokens:
    AB, C = 1664, 1024

    def __init__(self, g):
        self.g = g

    def rows(self, z0, nz):
        return pl.ds(pl.multiple_of(z0 * 8, 8), nz * 8)

    def ab(self, core, yy, xx, z0, nz):
        return self.g.at[core, yy, xx, self.rows(z0, nz), pl.ds(0, self.AB)]

    def c_block(self, core, yy, xx, zz):
        return self.g.at[core, yy, xx, self.rows(zz, 1), pl.ds(self.AB, self.C)]

    def c_row(self, core, yy, zz):
        return self.g.at[core, yy, :, self.rows(zz, 1), pl.ds(self.AB, self.C)]

    def c_slab(self, core, zz, part=None):
        ys = pl.ds(0, NY) if part is None else pl.ds(part * (NY // PARTS), NY // PARTS)
        return self.g.at[core, ys, :, self.rows(zz, 1), pl.ds(self.AB, self.C)]


def attend_part(
    post, q_ref, own_ref, block_ab_ref, block_c_ref, own_bias_ref, ab_bias_ref, c_bias_ref, out_ref,
    g_ab, g_c, top, total, acc, local_sem,
):
    def merge(keys, bias, first=False):
        q = q_ref[...]
        scores = lax.dot_general(q, keys, (((1,), (1,)), ((), ())), preferred_element_type=F32)
        rows, width = scores.shape
        scores = (scores.reshape(rows // 8, 8, width) * SCORE_SCALE + bias[None]).reshape(rows, width)
        best = jnp.max(scores, axis=1, keepdims=True)
        if not first:
            best = jnp.maximum(best, top[...])
        weights = jnp.exp(scores - best)
        summed = jnp.sum(weights, axis=1, keepdims=True)
        mixed = jnp.dot(weights.astype(BF16), keys[:, :LAT], preferred_element_type=F32)
        if first:
            total[...] = summed
            acc[...] = mixed
        else:
            scale = jnp.exp(top[...] - best)
            total[...] = total[...] * scale + summed
            acc[...] = acc[...] * scale + mixed
        top[...] = best

    pool = Pool(g_ab, g_c)
    block = block_ab_ref, block_c_ref
    started = False
    for parts in gather(post, block, pool, local_sem):
        if not started:
            merge(own_ref[...], own_bias_ref[...], first=True)
            started = True
        for part in parts:
            if len(part) == 2:
                yy, xx = part
                keys = jnp.concatenate([g_ab[h, yy, xx].reshape(NZ * Pool.AB, KPAD) for h in range(2)], axis=0)
                merge(keys, ab_bias_ref[yy * NX + xx])
            else:
                keys = jnp.concatenate([g_c[0, part[0]], g_c[1, part[0]]], axis=0)
                merge(keys, c_bias_ref[part[0]])
    out_ref[...] = (acc[...] / total[...]).reshape(out_ref.shape).astype(BF16)


def both_halves(v, c):
    v = jnp.concatenate([v, v], axis=0)
    return jnp.where(lax.broadcasted_iota(jnp.int32, v.shape, 0) // 4 == c, v, 0.0)


def own_rows(out_ref, halves, c):
    upper = lax.broadcasted_iota(jnp.int32, (4, HALF), 0) * 0 + c == 0
    for h in range(2):
        out_ref[:, h * HALF : (h + 1) * HALF] = jnp.where(upper, halves[h, :4], halves[h, 4:])


def project_part(
    ctx_ref, up_ref, hidden_ref, gain_ref, norm_ref,
    ctx_in, proj, other, from_other, parts, parts_in, full, res_ref, loads,
    local_sem, ctx_send, ctx_recv, send, recv, sib_send, sib_recv,
):
    z, y, x, c = here()
    e = (y * NX + x) * 2 + c
    chip = y * NX + x
    devices = 2 * NX * NY
    chips = NX * NY

    def ctx_copy(j):
        to = lax.rem(e + j, devices)
        return pltpu.make_async_remote_copy(
            src_ref=ctx_ref.at[to], dst_ref=ctx_in.at[e], send_sem=ctx_send.at[j], recv_sem=ctx_recv.at[j],
            device_id=(z, to), device_id_type=MESH,
        )

    def ctx_arrival(j):
        source = lax.rem(e - j + devices, devices)
        return pltpu.make_async_remote_copy(
            src_ref=ctx_in.at[source], dst_ref=ctx_in.at[source], send_sem=ctx_send.at[j],
            recv_sem=ctx_recv.at[j], device_id=(z, source), device_id_type=MESH,
        )

    def each(low, high, act):
        def body(j, carry):
            act(j)
            return carry

        lax.fori_loop(low, high, body, 0)

    each(1, devices, lambda j: ctx_copy(j).start())
    mine = pltpu.make_async_copy(ctx_ref.at[e], ctx_in.at[e], local_sem)
    mine.start()
    mine.wait()
    for load in loads:
        load.wait()
    each(1, devices, lambda j: ctx_arrival(j).wait_recv())

    context = ctx_in[...].reshape(devices * 8, LAT)
    first = jnp.dot(context, up_ref[0], preferred_element_type=F32).reshape(chips, 16, 128)
    second = jnp.dot(context, up_ref[1], preferred_element_type=F32).reshape(chips, 16, 128)
    upper = lax.broadcasted_iota(jnp.int32, (chips, 8, 128), 1) < 4

    def swap(v):
        return jnp.concatenate([v[:, 4:], v[:, :4]], axis=1)

    left = jnp.where(upper, first[:, :8], swap(first[:, 8:]))
    right = jnp.where(upper, swap(second[:, :8]), second[:, 8:])
    values = jnp.concatenate([left, right], axis=2).reshape(chips * 8, 256).astype(BF16)

    tile = 640
    for i in range(HALF // tile):
        columns = pl.ds(i * tile, tile)
        part = jnp.dot(values, proj[1, :, columns], preferred_element_type=F32)
        other[:, :, columns] = part.reshape(chips, 8, tile).astype(BF16)
    hidden = both_halves(hidden_ref[...].astype(F32), c)
    first_half = lax.broadcasted_iota(jnp.int32, (8, HALF), 0) * 0 + c == 0
    hidden_own = jnp.where(first_half, hidden[:, :HALF], hidden[:, HALF:])
    hidden_other = jnp.where(first_half, hidden[:, HALF:], hidden[:, :HALF])
    other[chip] = (other[chip].astype(F32) + hidden_other).astype(BF16)
    sib = pltpu.make_async_remote_copy(
        src_ref=other, dst_ref=from_other, send_sem=sib_send.at[0], recv_sem=sib_recv.at[0],
        device_id=dev(z, y, x, 1 - c), device_id_type=MESH,
    )
    sib.start()
    for i in range(HALF // tile):
        columns = pl.ds(i * tile, tile)
        part = jnp.dot(values, proj[0, :, columns], preferred_element_type=F32)
        full[:, :, columns] = part.reshape(chips, 8, tile)
    sib.wait()

    def total(j, carry):
        full[j] = full[j] + from_other[j].astype(F32)
        parts[j] = full[j].astype(BF16)
        return carry

    lax.fori_loop(0, chips, total, 0)

    def part_copy(j):
        to = lax.rem(chip + j, chips)
        return pltpu.make_async_remote_copy(
            src_ref=parts.at[to], dst_ref=parts_in.at[j], send_sem=send.at[j], recv_sem=recv.at[j],
            device_id=(z, to * 2 + c), device_id_type=MESH,
        )

    each(1, chips, lambda j: part_copy(j).start())
    res_ref[c] = full[chip] + hidden_own
    each(1, chips, lambda j: part_copy(j).wait_recv())

    def gathered(j, carry):
        return carry + parts_in[j].astype(F32)

    res_ref[c] = lax.fori_loop(1, chips, gathered, res_ref[c])
    swap_copy = pltpu.make_async_remote_copy(
        src_ref=res_ref.at[c], dst_ref=res_ref.at[c], send_sem=sib_send.at[1], recv_sem=sib_recv.at[1],
        device_id=dev(z, y, x, 1 - c), device_id_type=MESH,
    )
    swap_copy.start()
    swap_in = pltpu.make_async_remote_copy(
        src_ref=res_ref.at[1 - c], dst_ref=res_ref.at[1 - c], send_sem=sib_send.at[1],
        recv_sem=sib_recv.at[1], device_id=dev(z, y, x, 1 - c), device_id_type=MESH,
    )
    swap_in.wait_recv()
    squares = sum(jnp.sum(res_ref[h] * res_ref[h], axis=1, keepdims=True) for h in range(2))
    scale = lax.rsqrt(squares * (1.0 / D) + NORM_EPS)
    norm_ref[...] = (res_ref[c] * scale * gain_ref[c].astype(F32)).astype(BF16)

    def finish():
        swap_copy.wait_send()
        each(1, devices, lambda j: ctx_copy(j).wait_send())
        each(1, chips, lambda j: part_copy(j).wait_send())

    return finish


def add(ref, *others):
    if len(ref.shape) > 2:
        for i in range(ref.shape[0]):
            add(ref.at[i], *[o.at[i] for o in others])
        return
    value = ref[...].astype(F32)
    for o in others:
        value = value + o[...].astype(F32)
    ref[...] = value.astype(BF16)


class Ring4:
    def __init__(self, post, block, into, pos, lo, hi, to):
        self.post, self.block, self.into, self.lo, self.hi = post, block, into, lo, hi
        self.pos, self.plus, self.minus, self.far_at = pos, step(pos, 1, 4), step(pos, -1, 4), step(pos, 2, 4)
        self.up, self.down = to(1), to(-1)

    def put(self, src, i, device):
        return self.post.put(src, self.into.at[i], device, self.into.at[i])

    def far(self):
        self.far_up = self.put(self.block(self.far_at, self.lo), 0, self.up)
        self.far_down = self.put(self.block(self.far_at, self.hi), 1, self.down)

    def near(self):
        self.free_up = self.put(self.block(self.plus, self.hi), 2, self.up)
        self.free_down = self.put(self.block(self.minus, self.lo), 3, self.down)

    def last(self):
        self.far_up()
        add(self.block(self.plus, self.lo), self.into.at[0])
        self.last_up = self.put(self.block(self.plus, self.lo), 4, self.up)
        self.far_down()
        add(self.block(self.minus, self.hi), self.into.at[1])
        self.last_down = self.put(self.block(self.minus, self.hi), 5, self.down)

    def finish(self):
        self.free_up()
        self.last_down()
        add(self.block(self.pos, self.hi), self.into.at[2], self.into.at[5])
        self.free_down()
        self.last_up()
        add(self.block(self.pos, self.lo), self.into.at[3], self.into.at[4])


def ring8(post, sums, into, z, y, x, c):
    up_to, down_to = dev(step(z, 1, NZ), y, x, c), dev(step(z, -1, NZ), y, x, c)
    count = 0

    def half(dz, h):
        return sums.at[step(z, dz, NZ), pl.ds(2 * h, 2)]

    def put(dz, h):
        nonlocal count
        i = count
        count += 1
        return post.put(half(dz, h), into.at[i], up_to if dz > 0 else down_to, into.at[i]), into.at[i]

    up, down = [None, None], [None, None]
    up[0] = put(4, 0)
    down[1] = post.put(half(4, 1), into.at[count], down_to, into.at[count]), into.at[count]
    count += 1
    up[1], down[0] = put(3, 1), put(-3, 0)
    yield
    for dz in (3, 2, 1):
        for h_up in (0, 1):
            reach = dz if h_up == 0 else dz - 1
            if reach == 0:
                continue
            h_down = 1 - h_up
            up[h_up][0]()
            add(half(reach, h_up), up[h_up][1])
            up[h_up] = put(reach, h_up)
            down[h_down][0]()
            add(half(-reach, h_down), down[h_down][1])
            down[h_down] = put(-reach, h_down)
            yield
    for h in (1, 0):
        up[h][0]()
        down[h][0]()
        add(sums.at[z, pl.ds(2 * h, 2)], up[h][1], down[h][1])


SUM_AB, SUM_C = 1536, 1024


def moe_part(
    post, norm_ref, ids_ref, gates_ref, out_ref,
    block_ab, block_c, g, gate_up, down, hidden, other, from_other, sums, other_c, from_c, sums_c,
    ring_a, ring_b, ring_c, ring_d, ring_z, row_in, block_in, z_in, final, loads, local_sem,
):
    z, y, x, c = here()
    lane = lax.broadcasted_iota(jnp.int32, (4, TABLE), 1)
    ids, gates = ids_ref[...], gates_ref[...].astype(F32)
    table = sum(jnp.where(ids[:, k : k + 1] == lane, gates[:, k : k + 1], 0.0) for k in range(ids.shape[1]))
    block_ab[...] = norm_ref[:, : Tokens.AB]
    block_c[:, : HALF - Tokens.AB] = norm_ref[:, Tokens.AB :]
    block_c[:, HALF - Tokens.AB :] = both_halves(table, c).astype(BF16)
    for _ in gather(post, (block_ab, block_c), Tokens(g), local_sem):
        pass
    for load in loads:
        load.wait()

    e = (y * NX + x) * 2 + c
    ours = (lax.broadcasted_iota(jnp.int32, (256, TABLE), 1) == e).astype(F32)

    def hidden_rows(i, carry):
        rows = [g[h, i].reshape(256, HALF + TABLE) for h in range(2)]
        weight = jnp.sum(
            (rows[0][:, HALF:].astype(F32) + rows[1][:, HALF:].astype(F32)) * ours, axis=1, keepdims=True
        )
        product = sum(
            lax.dot_general(
                rows[h][:, :HALF], gate_up[:, h * HALF : (h + 1) * HALF], (((1,), (1,)), ((), ())),
                preferred_element_type=F32,
            )
            for h in range(2)
        )
        gated, raised = product[:, :FFG], product[:, FFG:]
        hidden[i] = (gated / (1.0 + jnp.exp(-gated)) * raised * weight).astype(BF16).reshape(NX, 64, FFG)
        return carry

    lax.fori_loop(0, NY, hidden_rows, 0)

    xs = [step(x, o, NX) for o in range(NX)]
    ys = [step(y, o, NY) for o in range(NY)]
    tile = SUM_AB // 2
    twin = dev(z, y, x, 1 - c)

    def place(ref, name, o):
        if name == "a":
            return ref.at[ys[o], :, pl.ds(0, 32)]
        return ref.at[:, xs[o], pl.ds(32, 32)]

    def rows_of(name, o):
        return place(hidden, name, o)[...].reshape(128, FFG)

    def columns_c(i, rows):
        return jnp.dot(rows, down[i, :, SUM_AB:], preferred_element_type=F32).reshape(NX, NZ, 8, SUM_C)

    arrive = {}

    def give(name, o):
        rows = rows_of(name, o)
        for i in range(2):
            columns = pl.ds(i * tile, tile)
            part = jnp.dot(rows, down[1, :, columns], preferred_element_type=F32)
            place(other, name, o).at[:, :, columns][...] = part.reshape(4, 32, tile).astype(BF16)
        arrive[(name, o)] = post.put(place(other, name, o), place(from_other, name, o), twin, place(from_other, name, o))

    def take(name, o):
        arrive[(name, o)]()
        rows = rows_of(name, o)
        for i in range(2):
            columns = pl.ds(i * tile, tile)
            part = jnp.dot(rows, down[0, :, columns], preferred_element_type=F32).reshape(4, 32, tile)
            theirs = place(from_other, name, o).at[:, :, columns][...].astype(F32)
            place(sums, name, o).at[:, :, columns][...] = (part + theirs).astype(BF16)

    def give_c(i, carry):
        part = columns_c(1, hidden[i].reshape(256, FFG))
        for xx in range(NX):
            other_c[:, i, xx] = part[xx].astype(BF16)
        return carry

    def take_c(i, carry):
        part = columns_c(0, hidden[i].reshape(256, FFG))
        for xx in range(NX):
            sums_c[:, i, xx] = (part[xx] + from_c[:, i, xx].astype(F32)).astype(BF16)
        return carry

    a_lo, a_hi, b_lo, b_hi = [pl.ds(16 * i, 16) for i in range(4)]

    def to_x(s):
        return dev(z, y, step(x, s, NX), c)

    def to_y(s):
        return dev(z, step(y, s, NY), x, c)

    first = (
        Ring4(post, lambda p, r: sums.at[p, :, r], ring_a, y, a_lo, a_hi, to_y),
        Ring4(post, lambda p, r: sums.at[:, p, r], ring_b, x, b_lo, b_hi, to_x),
    )
    second = (
        Ring4(post, lambda p, r: sums.at[y, p, r], ring_c, x, a_lo, a_hi, to_x),
        Ring4(post, lambda p, r: sums.at[p, x, r], ring_d, y, b_lo, b_hi, to_y),
    )
    along_z = ring8(post, sums_c, ring_z, z, y, x, c)

    for o in (2, 1, 3):
        give("a", o)
        give("b", o)
    take("a", 2)
    take("b", 2)
    for ring in first:
        ring.far()
    lax.fori_loop(0, NY, give_c, 0)
    arrive_c = post.put(other_c, from_c, twin, from_c)
    for o in (1, 3):
        take("a", o)
        take("b", o)
    for ring in first:
        ring.near()
    give("a", 0)
    give("b", 0)
    arrive_c()
    lax.fori_loop(0, NY, take_c, 0)
    next(along_z)
    for ring in first:
        ring.last()
    take("a", 0)
    take("b", 0)
    next(along_z)
    next(along_z)
    for ring in first:
        ring.finish()
    for ring in second:
        ring.far()
        ring.near()
    next(along_z)
    for ring in second:
        ring.last()
    next(along_z)
    for ring in second:
        ring.finish()

    def zrows(at):
        return pl.ds(pl.multiple_of(at * 8, 8), 8)

    waits = [
        post.put(sums.at[y, x, zrows(step(z, j, NZ))], z_in.at[j], dev(step(z, j, NZ), y, x, c), z_in.at[j])
        for j in (1, 7, 2, 6, 3, 5, 4)
    ]
    keep = pltpu.make_async_copy(sums.at[y, x, zrows(z)], z_in.at[0], local_sem.at[0])
    keep.start()
    for _ in along_z:
        pass
    row_waits = [
        post.put(sums_c.at[z, step(y, o, NY)], row_in.at[o], to_y(o), row_in.at[o]) for o in (1, 3, 2)
    ]
    for wait in row_waits:
        wait()
    add(sums_c.at[z, y], *[row_in.at[o] for o in (1, 2, 3)])
    block_waits = [
        post.put(sums_c.at[z, y, step(x, o, NX)], block_in.at[o], to_x(o), block_in.at[o]) for o in (1, 3, 2)
    ]
    keep.wait()
    for wait in waits:
        wait()
    value = z_in[0].astype(F32)
    for j in range(1, NZ):
        value = value + z_in[j].astype(F32)
    final[c, :, :SUM_AB] = value
    for wait in block_waits:
        wait()
    value = sums_c[z, y, x].astype(F32)
    for o in range(1, 4):
        value = value + block_in[o].astype(F32)
    final[c, :, SUM_AB:] = value
    post.put(final.at[c], final.at[c], twin, final.at[1 - c])()
    own_rows(out_ref, final, c)


def layer_kernel(
    q_ref, own_ref, block_ab_ref, block_c_ref, own_bias_ref, ab_bias_ref, c_bias_ref,
    value_up_ref, hidden_ref, gain_ref, ids_ref, gates_ref, proj_hbm, gate_hbm, up_hbm, down_hbm,
    res_ref, out_ref,
    pool_ab, pool_c, top, total, acc, ctx,
    ctx_in, proj, p_other, p_from, parts, parts_in, full, residual, normed,
    block_ab, block_c, g, gate_up, down, hidden, other, from_other, sums, other_c, from_c, sums_c,
    ring_a, ring_b, ring_c, ring_d, ring_z, row_in, block_in, z_in, final,
    send, recv, local_sem, load_sem, ctx_send, ctx_recv, part_send, part_recv, sib_send, sib_recv,
):
    z, y, x, c = here()
    devices = 2 * NX * NY
    e = (y * NX + x) * 2 + c

    def column_half(half):
        return pl.ds(pl.multiple_of(half * HALF, 128), HALF)

    pairs = [(proj_hbm.at[:, column_half(half)], proj.at[i]) for i, half in enumerate((c, 1 - c))]
    pairs += [(gate_hbm.at[0], gate_up.at[pl.ds(0, FFG)]), (up_hbm.at[0], gate_up.at[pl.ds(FFG, FFG)])]
    pairs += [(down_hbm.at[0, :, column_half(half)], down.at[i]) for i, half in enumerate((c, 1 - c))]
    loads = [pltpu.make_async_copy(src, dst, load_sem.at[i]) for i, (src, dst) in enumerate(pairs)]
    for load in loads:
        load.start()

    barrier = pltpu.get_barrier_semaphore()

    def hello(j, carry):
        pl.semaphore_signal(
            barrier, inc=1, device_id=(z, lax.rem(e + j, devices)), device_id_type=MESH
        )
        return carry

    lax.fori_loop(1, devices, hello, 0)
    for j in range(1, NZ):
        pl.semaphore_signal(barrier, inc=1, device_id=dev(step(z, j, NZ), y, x, c), device_id_type=MESH)
    pl.semaphore_wait(barrier, devices - 1 + NZ - 1)

    post = Post(send, recv)
    attend_part(
        post, q_ref, own_ref, block_ab_ref, block_c_ref, own_bias_ref, ab_bias_ref, c_bias_ref, ctx,
        pool_ab, pool_c, top, total, acc, local_sem,
    )
    finish = project_part(
        ctx, value_up_ref, hidden_ref, gain_ref, normed,
        ctx_in, proj, p_other, p_from, parts, parts_in, full, residual, loads[:2],
        local_sem.at[0], ctx_send, ctx_recv, part_send, part_recv, sib_send, sib_recv,
    )
    moe_part(
        post, normed, ids_ref, gates_ref, out_ref,
        block_ab, block_c, g, gate_up, down, hidden, other, from_other, sums, other_c, from_c, sums_c,
        ring_a, ring_b, ring_c, ring_d, ring_z, row_in, block_in, z_in, final, loads[2:], local_sem,
    )
    own_rows(res_ref, residual, c)
    finish()
    post.drain()


def layer(*operands):
    vmem = pl.BlockSpec(memory_space=pltpu.VMEM)
    hbm = pl.BlockSpec(memory_space=pl.ANY)
    chips, rows = NX * NY, 256
    return pl.pallas_call(
        layer_kernel,
        out_shape=(jax.ShapeDtypeStruct((4, D), F32), jax.ShapeDtypeStruct((4, D), F32)),
        in_specs=[vmem] * 12 + [hbm] * 4,
        out_specs=(vmem, vmem),
        scratch_shapes=[
            pltpu.VMEM((2, NY, NX, NZ, Pool.AB, KPAD), BF16),
            pltpu.VMEM((2, NZ, Pool.C, KPAD), BF16),
            pltpu.VMEM((rows, 1), F32),
            pltpu.VMEM((rows, 1), F32),
            pltpu.VMEM((rows, LAT), F32),
            pltpu.VMEM((2 * chips, 8, LAT), BF16),
            pltpu.VMEM((2 * chips, 8, LAT), BF16),
            pltpu.VMEM((2, 256, HALF), BF16),
            pltpu.VMEM((chips, 8, HALF), BF16),
            pltpu.VMEM((chips, 8, HALF), BF16),
            pltpu.VMEM((chips, 8, HALF), BF16),
            pltpu.VMEM((chips, 8, HALF), BF16),
            pltpu.VMEM((chips, 8, HALF), F32),
            pltpu.VMEM((2, 8, HALF), F32),
            pltpu.VMEM((8, HALF), BF16),
            pltpu.VMEM((8, Tokens.AB), BF16),
            pltpu.VMEM((8, Tokens.C), BF16),
            pltpu.VMEM((2, NY, NX, NZ * 8, HALF + TABLE), BF16),
            pltpu.VMEM((2 * FFG, D), BF16),
            pltpu.VMEM((2, FFG, HALF), BF16),
            pltpu.VMEM((NY, NX, 64, FFG), BF16),
            pltpu.VMEM((NY, NX, 64, SUM_AB), BF16),
            pltpu.VMEM((NY, NX, 64, SUM_AB), BF16),
            pltpu.VMEM((NY, NX, 64, SUM_AB), BF16),
            pltpu.VMEM((NZ, NY, NX, 8, SUM_C), BF16),
            pltpu.VMEM((NZ, NY, NX, 8, SUM_C), BF16),
            pltpu.VMEM((NZ, NY, NX, 8, SUM_C), BF16),
            pltpu.VMEM((6, NX, 16, SUM_AB), BF16),
            pltpu.VMEM((6, NY, 16, SUM_AB), BF16),
            pltpu.VMEM((6, 16, SUM_AB), BF16),
            pltpu.VMEM((6, 16, SUM_AB), BF16),
            pltpu.VMEM((14, NY // 2, NX, 8, SUM_C), BF16),
            pltpu.VMEM((4, NX, 8, SUM_C), BF16),
            pltpu.VMEM((4, 8, SUM_C), BF16),
            pltpu.VMEM((NZ, 8, SUM_AB), BF16),
            pltpu.VMEM((2, 8, HALF), F32),
            pltpu.SemaphoreType.DMA((COPIES,)),
            pltpu.SemaphoreType.DMA((COPIES,)),
            pltpu.SemaphoreType.DMA((2,)),
            pltpu.SemaphoreType.DMA((6,)),
            pltpu.SemaphoreType.DMA((2 * chips,)),
            pltpu.SemaphoreType.DMA((2 * chips,)),
            pltpu.SemaphoreType.DMA((chips,)),
            pltpu.SemaphoreType.DMA((chips,)),
            pltpu.SemaphoreType.DMA((2,)),
            pltpu.SemaphoreType.DMA((2,)),
        ],
        compiler_params=pltpu.CompilerParams(
            collective_id=0, has_side_effects=True, vmem_limit_bytes=60 * 2**20
        ),
        name="layer",
    )(*operands)


def per_device(
    hidden_in, query, prefix_pool, suffix_cache, block_list, prefix_count, suffix_count, value_up,
    out_proj, norm_gain, expert_ids, gate_weights, gate_proj, up_proj, down_proj,
):
    e = lax.axis_index("expert")
    core, chip = lax.rem(e, 2), lax.div(e, 2)

    def padded(v):
        return jnp.pad(v, ((0, 0), (0, KPAD - KDIM)))

    block_ab = lax.dynamic_slice(prefix_pool, (chip, core * (24 * KDIM)), (1, 24 * KDIM))
    block_ab = padded(block_ab.reshape(24, KDIM))[None]
    block_c = lax.dynamic_slice(prefix_pool, (core * 8, 48 * KDIM), (8, 16 * KDIM))
    block_c = padded(block_c.reshape(128, KDIM))
    q = query.reshape(4, 32, 2, KDIM).transpose(1, 2, 0, 3).reshape(256, KDIM)
    q = jnp.pad(q, ((0, 0), (0, KPAD - KDIM)))
    own = jnp.pad(suffix_cache.reshape(4 * SUFFIX, KDIM), ((0, 0), (0, KPAD - KDIM)))
    in_prefix = jnp.arange(32, dtype=jnp.int32)[None, :] < prefix_count[:, None]
    listed = jnp.where(in_prefix, block_list, -1)
    member = jnp.any(listed[:, :, None] == jnp.arange(128, dtype=jnp.int32), axis=1)
    member = member.reshape(4, NZ, 16).transpose(2, 0, 1)
    member = jnp.where(member, 0.0, NEG_FILL).astype(F32)
    ab_bias = jnp.broadcast_to(
        member[:, None, :, None, :, None], (16, 2, 4, 2, NZ, Pool.AB)
    ).reshape(16, 8, 2 * NZ * Pool.AB)
    c_bias = jnp.broadcast_to(
        member.transpose(2, 1, 0)[:, None, :, :, None], (NZ, 2, 4, 16, 16)
    ).reshape(NZ, 8, 2 * Pool.C)
    row = jnp.arange(4 * SUFFIX, dtype=jnp.int32)
    own_live = (row // SUFFIX == jnp.arange(4, dtype=jnp.int32)[:, None]) & (
        row % SUFFIX < suffix_count[:, None]
    )
    own_live = jnp.concatenate([own_live, own_live], axis=0)
    own_bias = jnp.where(own_live, 0.0, NEG_FILL).astype(F32)
    return layer(
        q, own, block_ab, block_c, own_bias, ab_bias, c_bias,
        value_up, hidden_in, norm_gain.reshape(2, 1, HALF), expert_ids, gate_weights,
        out_proj, gate_proj.transpose(0, 2, 1), up_proj.transpose(0, 2, 1), down_proj,
    )


def solution(mesh):
    rows = P(("dp", "expert"), None)
    in_specs = (
        rows, rows, P("dp", None), rows, rows, P(("dp", "expert")), P(("dp", "expert")),
        P("expert", None, None), P("expert", None), P(), rows, rows,
        P("expert", None, "dp"), P("expert", None, "dp"), P("expert", "dp", None),
    )
    return jax.shard_map(
        per_device, mesh=mesh, in_specs=in_specs, out_specs=(rows, rows), check_vma=False
    )
```

```python
import functools
import jax
import jax.numpy as jnp
from jax import lax
from jax.experimental import pallas as pl
from jax.experimental.pallas import tpu as pltpu
from jax.sharding import PartitionSpec as P

HEADS = 64
LAT = 512
BLOCK = 64
SUFFIX = 128
KDIM = 576
D = 5120
HALF = 2560
FFG = 192
TABLE = 128

NEG_FILL = -1e30
SCORE_SCALE = 192.0 ** (-0.5)
NORM_EPS = 1e-06
LOG2_E = 1.4426950408889634

NX, NY, NZ = 4, 4, 8
MESH = pl.DeviceIdType.MESH
F32 = jnp.float32
BF16 = jnp.bfloat16


def here():
    z = lax.axis_index("dp")
    e = lax.axis_index("expert")
    core = lax.rem(e, 2)
    chip = lax.div(e, 2)
    return z, lax.div(chip, NX), lax.rem(chip, NX), core


def dev(z, y, x, core):
    return (z, (y * NX + x) * 2 + core)


def step(v, by, n):
    return lax.rem(v + by + n, n)


class Post:
    def __init__(self, send, recv):
        self.send, self.recv, self.count, self.sent = send, recv, 0, []

    def put(self, src, dst, to, lands):
        i = self.count
        self.count += 1
        copy = pltpu.make_async_remote_copy(
            src_ref=src, dst_ref=dst, send_sem=self.send.at[i], recv_sem=self.recv.at[i],
            device_id=to, device_id_type=MESH,
        )
        copy.start()
        self.sent.append(copy)
        return pltpu.make_async_remote_copy(
            src_ref=lands, dst_ref=lands, send_sem=self.send.at[i], recv_sem=self.recv.at[i],
            device_id=to, device_id_type=MESH,
        ).wait_recv

    def drain(self):
        for copy in self.sent:
            copy.wait_send()


def gather(post, block, g, local_sem):
    z, y, x, c = here()
    xs = {o: step(x, o, NX) for o in (0, -1, 1, 2)}
    ys = {o: step(y, o, NY) for o in (0, -1, 1, 2)}
    zs = {o: step(z, o, NZ) for o in range(-4, 5)}
    other = dev(z, y, x, 1 - c)

    def move(view, arriving, to):
        return post.put(view, view, to, arriving)

    block_ab, block_c = block
    whole = g.c_block is None
    keeps = [
        pltpu.make_async_copy(block_ab, g.ab(c, y, x, z, 1), local_sem.at[0]),
        pltpu.make_async_copy(block_c, g.c_slab(c, z) if whole else g.c_block(c, y, x, z), local_sem.at[1]),
    ]
    for keep in keeps:
        keep.start()
    c_x = [] if whole else [
        post.put(block_c, g.c_block(c, y, x, z), dev(z, y, step(x, o, NX), c), g.c_block(c, y, step(x, -o, NX), z))
        for o in (1, 3, 2)
    ]
    ab_z = [
        post.put(block_ab, g.ab(c, y, x, z, 1), dev(step(z, j, NZ), y, x, c), g.ab(c, y, x, step(z, -j, NZ), 1))
        for j in (1, 7, 2, 6, 3, 5, 4)
    ]
    for keep in keeps:
        keep.wait()
    from_sibling = {}

    def sibling_c(dz):
        from_sibling[dz] = move(g.c_slab(c, zs[dz]), g.c_slab(1 - c, zs[dz]), other)

    def along_z(dz, by, part):
        return move(g.c_slab(c, zs[dz], part), g.c_slab(c, zs[dz - by], part), dev(zs[by], y, x, c))

    up, down = {}, {}

    def begin_z():
        for part in range(PARTS):
            up[part], down[PARTS - 1 - part] = along_z(0, 1, part), along_z(0, -1, PARTS - 1 - part)
        sibling_c(0)

    ring_events = [(s, part) for s in (1, 2, 3) for part in range(PARTS)]

    def ring_z(events):
        for _ in range(events):
            s, part = ring_events.pop(0)
            up[part]()
            if s < 3 or part < PARTS // 2:
                up[part] = along_z(-s, 1, part)
            back = PARTS - 1 - part
            down[back]()
            if s < 3 or back >= PARTS // 2:
                down[back] = along_z(s, -1, back)
            if part == PARTS - 1:
                sibling_c(-s)
                sibling_c(s)

    for wait in c_x:
        wait()
    c_y = [] if whole else [
        move(g.c_row(c, y, z), g.c_row(c, step(y, -o, NY), z), dev(z, step(y, o, NY), x, c)) for o in (1, 3, 2)
    ]
    if whole:
        begin_z()
    yield []
    for wait in ab_z:
        wait()

    halves = {"a": (0, 4), "b": (4, 4), "a_lo": (0, 2), "a_hi": (2, 2), "b_lo": (4, 2), "b_hi": (6, 2)}
    def sibling(name, dy, dx):
        yy, xx = ys[dy], xs[dx]
        from_sibling[(name, dy, dx)] = move(g.ab(c, yy, xx, *halves[name]), g.ab(1 - c, yy, xx, *halves[name]), other)

    def along_x(dy, dx, name, by):
        yy, xx = ys[dy], xs[dx]
        return move(
            g.ab(c, yy, xx, *halves[name]), g.ab(c, yy, step(xx, -by, NX), *halves[name]), dev(z, y, xs[by], c)
        )

    def along_y(dy, dx, name, by):
        yy, xx = ys[dy], xs[dx]
        return move(
            g.ab(c, yy, xx, *halves[name]), g.ab(c, step(yy, -by, NY), xx, *halves[name]), dev(z, ys[by], x, c)
        )

    a1p, b1p = along_x(0, 0, "a", 1), along_y(0, 0, "b", 1)
    a1m, b1m = along_x(0, 0, "a", -1), along_y(0, 0, "b", -1)
    sibling("a", 0, 0)
    sibling("b", 0, 0)
    a2, b2 = {}, {}

    def second(o):
        a2[o] = (along_y(0, o, "a", 1), along_y(0, o, "a", -1))
        b2[o] = (along_x(o, 0, "b", 1), along_x(o, 0, "b", -1))

    second(0)
    if not whole:
        for wait in c_y:
            wait()
        begin_z()
    else:
        ring_z(PARTS)
    a1p()
    fa_lo = along_x(0, -1, "a_lo", 1)
    b1p()
    fb_lo = along_y(-1, 0, "b_lo", 1)
    a1m()
    fa_hi = along_x(0, 1, "a_hi", -1)
    b1m()
    fb_hi = along_y(1, 0, "b_hi", -1)
    for o in (-1, 1):
        second(o)
        sibling("a", 0, o)
        sibling("b", o, 0)

    def done(*parts):
        ready = []
        for part in parts:
            if isinstance(part, int):
                from_sibling[part]()
                ready.append((zs[part],))
            else:
                from_sibling[("a",) + part]()
                from_sibling[("b",) + part]()
                ready.append((ys[part[0]], xs[part[1]]))
        return ready

    queue = [(0, 0), 0]

    def some():
        return done(queue.pop(0)) if queue else []

    yield some()
    ring_z(PARTS)
    yield some()
    fa_lo()
    fa_hi()
    fb_lo()
    fb_hi()
    second(2)
    sibling("a", 0, 2)
    sibling("b", 2, 0)

    last_a, last_b = {}, {}
    ready = {
        0: [(-1, 0), (1, 0), (0, -1), (0, 1)], -1: [(-1, -1)], 1: [(1, 1), (1, -1), (-1, 1)], 2: [],
    }
    seen = 0
    for o in (0, -1, 1, 2):
        ring_z(min(PARTS // 2, len(ring_events)))
        yield some()
        a2[o][0]()
        lo_a = along_y(-1, o, "a_lo", 1)
        b2[o][0]()
        lo_b = along_x(o, -1, "b_lo", 1)
        yield some()
        a2[o][1]()
        last_a[o] = (lo_a, along_y(1, o, "a_hi", -1))
        b2[o][1]()
        last_b[o] = (lo_b, along_x(o, 1, "b_hi", -1))
        for side in (-1, 1):
            sibling("a", side, o)
            sibling("b", o, side)
        yield some()
        now = 3 - -(-len(ring_events) // PARTS)
        queue += ready[o] + [d for n in range(seen + 1, now + 1) for d in (-n, n)]
        seen = now
    for o in (0, -1, 1, 2):
        for wait in last_a[o]:
            wait()
        sibling("a", 2, o)
        yield some()
        for wait in last_b[o]:
            wait()
        sibling("b", o, 2)
        yield some()
        queue += [(2, o), (o, 2)] if o != 2 else [(2, 2)]
    for part in range(PARTS // 2):
        up[part]()
        down[PARTS - 1 - part]()
    sibling_c(4)
    queue += [4]
    while queue:
        yield some()


COPIES = 400
PARTS = 4


class Pool:
    AB, C = 24, 128
    c_block = None

    def __init__(self, ab, c):
        self.g_ab, self.g_c = ab, c

    def ab(self, core, yy, xx, z0, nz):
        return self.g_ab.at[core, yy, xx, pl.ds(z0, nz)]

    def c_slab(self, core, zz, part=None):
        if part is None:
            return self.g_c.at[core, zz]
        return self.g_c.at[core, zz, pl.ds(part * (self.C // PARTS), self.C // PARTS)]


class Tokens:
    AB, C = 1664, 1024

    def __init__(self, g):
        self.g = g

    def rows(self, z0, nz):
        return pl.ds(pl.multiple_of(z0 * 8, 8), nz * 8)

    def ab(self, core, yy, xx, z0, nz):
        return self.g.at[core, yy, xx, self.rows(z0, nz), pl.ds(0, self.AB)]

    def c_block(self, core, yy, xx, zz):
        return self.g.at[core, yy, xx, self.rows(zz, 1), pl.ds(self.AB, self.C)]

    def c_row(self, core, yy, zz):
        return self.g.at[core, yy, :, self.rows(zz, 1), pl.ds(self.AB, self.C)]

    def c_slab(self, core, zz, part=None):
        ys = pl.ds(0, NY) if part is None else pl.ds(part * (NY // PARTS), NY // PARTS)
        return self.g.at[core, ys, :, self.rows(zz, 1), pl.ds(self.AB, self.C)]


def attend_part(
    post, q_ref, own_ref, block_ab_ref, block_c_ref, list_ref, prefix_ref, suffix_ref, out_ref,
    g_ab, g_c, top, total, acc, local_sem,
):
    def request(shape):
        return lax.rem(lax.broadcasted_iota(jnp.int32, shape, 0), 4)

    def by_request(ref, shape):
        turn = request(shape)
        return jnp.where(turn == 0, ref[0], jnp.where(turn == 1, ref[1], jnp.where(turn == 2, ref[2], ref[3])))

    def live_bias(live):
        return (live.astype(F32) - 1.0) * -NEG_FILL

    def member_blocks():
        listed = jnp.concatenate([list_ref[...], list_ref[...]], axis=0)
        block, count = lax.broadcasted_iota(jnp.int32, (8, 128), 1), by_request(prefix_ref, (8, 128))
        member = jnp.zeros((8, 128), F32)
        for j in range(listed.shape[1]):
            member = jnp.where((listed[:, j : j + 1] == block) & (j < count), 1.0, member)
        return member.astype(BF16)

    def own_bias():
        shape = (8, 4 * SUFFIX)
        row = lax.broadcasted_iota(jnp.int32, shape, 1)
        place = row - SUFFIX * request(shape)
        return live_bias(jnp.where((place >= 0) & (place < by_request(suffix_ref, shape)), 1.0, 0.0))

    def pool_bias(member, block_of_key):
        block = lax.broadcasted_iota(jnp.int32, block_of_key.shape, 0)
        spread = jnp.where(block == block_of_key, 1.0, 0.0).astype(BF16)
        return live_bias(jnp.dot(member, spread, preferred_element_type=F32))

    def ab_bias(member, k):
        key = lax.broadcasted_iota(jnp.int32, (128, 2 * NZ * Pool.AB), 1)
        zz = sum((key >= Pool.AB * i).astype(jnp.int32) for i in range(1, 2 * NZ))
        return pool_bias(member, (zz - jnp.where(zz >= NZ, NZ, 0)) * 16 + k)

    def c_bias(member, zz):
        key = lax.broadcasted_iota(jnp.int32, (128, 2 * Pool.C), 1)
        return pool_bias(member, lax.shift_right_logical(key, 4) + zz * 16)

    def merge(keys, bias, first=False):
        q = q_ref[...]
        scores = lax.dot_general(q, keys, (((1,), (1,)), ((), ())), preferred_element_type=F32)
        rows, width = scores.shape
        scores = (scores.reshape(rows // 8, 8, width) * (SCORE_SCALE * LOG2_E) + bias[None]).reshape(rows, width)
        best = jnp.max(scores, axis=1, keepdims=True)
        if not first:
            best = jnp.maximum(best, top[...])
        weights = jnp.exp2(scores - best)
        summed = jnp.sum(weights, axis=1, keepdims=True)
        mixed = jnp.dot(weights.astype(BF16), keys[:, :LAT], preferred_element_type=F32)
        if first:
            total[...] = summed
            acc[...] = mixed
        else:
            scale = jnp.exp2(top[...] - best)
            total[...] = total[...] * scale + summed
            acc[...] = acc[...] * scale + mixed
        top[...] = best

    pool = Pool(g_ab, g_c)
    block = block_ab_ref, block_c_ref
    started = False
    for parts in gather(post, block, pool, local_sem):
        if not started:
            merge(own_ref[...], own_bias(), first=True)
            member = member_blocks()
            started = True
        for part in parts:
            if len(part) == 2:
                yy, xx = part
                keys = jnp.concatenate([g_ab[h, yy, xx].reshape(NZ * Pool.AB, KDIM) for h in range(2)], axis=0)
                merge(keys, ab_bias(member, yy * NX + xx))
            else:
                keys = jnp.concatenate([g_c[0, part[0]], g_c[1, part[0]]], axis=0)
                merge(keys, c_bias(member, part[0]))
    out_ref[...] = (acc[...] / total[...]).reshape(out_ref.shape).astype(BF16)


def both_halves(v, c):
    v = jnp.concatenate([v, v], axis=0)
    return jnp.where(lax.broadcasted_iota(jnp.int32, v.shape, 0) // 4 == c, v, 0.0)


def own_rows(out_ref, halves, c):
    upper = lax.broadcasted_iota(jnp.int32, (4, HALF), 0) * 0 + c == 0
    for h in range(2):
        out_ref[:, h * HALF : (h + 1) * HALF] = jnp.where(upper, halves[h, :4], halves[h, 4:])


def project_part(
    ctx_ref, up_ref, hidden_ref, gain_ref, norm_ref,
    ctx_in, proj, other, from_other, parts, parts_in, full, res_ref, loads,
    local_sem, ctx_send, ctx_recv, send, recv, sib_send, sib_recv,
):
    z, y, x, c = here()
    e = (y * NX + x) * 2 + c
    chip = y * NX + x
    devices = 2 * NX * NY
    chips = NX * NY

    def ctx_copy(j):
        to = lax.rem(e + j, devices)
        return pltpu.make_async_remote_copy(
            src_ref=ctx_ref.at[to], dst_ref=ctx_in.at[e], send_sem=ctx_send.at[j], recv_sem=ctx_recv.at[j],
            device_id=(z, to), device_id_type=MESH,
        )

    def ctx_arrival(j):
        source = lax.rem(e - j + devices, devices)
        return pltpu.make_async_remote_copy(
            src_ref=ctx_in.at[source], dst_ref=ctx_in.at[source], send_sem=ctx_send.at[j],
            recv_sem=ctx_recv.at[j], device_id=(z, source), device_id_type=MESH,
        )

    def each(low, high, act):
        def body(j, carry):
            act(j)
            return carry

        lax.fori_loop(low, high, body, 0)

    each(1, devices, lambda j: ctx_copy(j).start())
    mine = pltpu.make_async_copy(ctx_ref.at[e], ctx_in.at[e], local_sem)
    mine.start()
    mine.wait()
    for load in loads:
        load.wait()
    each(1, devices, lambda j: ctx_arrival(j).wait_recv())

    context = ctx_in[...].reshape(devices * 8, LAT)
    first = jnp.dot(context, up_ref[0], preferred_element_type=F32).reshape(chips, 16, 128)
    second = jnp.dot(context, up_ref[1], preferred_element_type=F32).reshape(chips, 16, 128)
    upper = lax.broadcasted_iota(jnp.int32, (chips, 8, 128), 1) < 4

    def swap(v):
        return jnp.concatenate([v[:, 4:], v[:, :4]], axis=1)

    left = jnp.where(upper, first[:, :8], swap(first[:, 8:]))
    right = jnp.where(upper, swap(second[:, :8]), second[:, 8:])
    values = jnp.concatenate([left, right], axis=2).reshape(chips * 8, 256).astype(BF16)

    tile = 640
    for i in range(HALF // tile):
        columns = pl.ds(i * tile, tile)
        part = jnp.dot(values, proj[1, :, columns], preferred_element_type=F32)
        other[:, :, columns] = part.reshape(chips, 8, tile).astype(BF16)
    hidden = both_halves(hidden_ref[...].astype(F32), c)
    first_half = lax.broadcasted_iota(jnp.int32, (8, HALF), 0) * 0 + c == 0
    hidden_own = jnp.where(first_half, hidden[:, :HALF], hidden[:, HALF:])
    hidden_other = jnp.where(first_half, hidden[:, HALF:], hidden[:, :HALF])
    other[chip] = (other[chip].astype(F32) + hidden_other).astype(BF16)
    sib = pltpu.make_async_remote_copy(
        src_ref=other, dst_ref=from_other, send_sem=sib_send.at[0], recv_sem=sib_recv.at[0],
        device_id=dev(z, y, x, 1 - c), device_id_type=MESH,
    )
    sib.start()
    for i in range(HALF // tile):
        columns = pl.ds(i * tile, tile)
        part = jnp.dot(values, proj[0, :, columns], preferred_element_type=F32)
        full[:, :, columns] = part.reshape(chips, 8, tile)
    sib.wait()

    def total(j, carry):
        full[j] = full[j] + from_other[j].astype(F32)
        parts[j] = full[j].astype(BF16)
        return carry

    lax.fori_loop(0, chips, total, 0)

    def part_copy(j):
        to = lax.rem(chip + j, chips)
        return pltpu.make_async_remote_copy(
            src_ref=parts.at[to], dst_ref=parts_in.at[j], send_sem=send.at[j], recv_sem=recv.at[j],
            device_id=(z, to * 2 + c), device_id_type=MESH,
        )

    each(1, chips, lambda j: part_copy(j).start())
    res_ref[c] = full[chip] + hidden_own
    each(1, chips, lambda j: part_copy(j).wait_recv())

    def gathered(j, carry):
        return carry + parts_in[j].astype(F32)

    res_ref[c] = lax.fori_loop(1, chips, gathered, res_ref[c])
    swap_copy = pltpu.make_async_remote_copy(
        src_ref=res_ref.at[c], dst_ref=res_ref.at[c], send_sem=sib_send.at[1], recv_sem=sib_recv.at[1],
        device_id=dev(z, y, x, 1 - c), device_id_type=MESH,
    )
    swap_copy.start()
    swap_in = pltpu.make_async_remote_copy(
        src_ref=res_ref.at[1 - c], dst_ref=res_ref.at[1 - c], send_sem=sib_send.at[1],
        recv_sem=sib_recv.at[1], device_id=dev(z, y, x, 1 - c), device_id_type=MESH,
    )
    swap_in.wait_recv()
    squares = sum(jnp.sum(res_ref[h] * res_ref[h], axis=1, keepdims=True) for h in range(2))
    scale = lax.rsqrt(squares * (1.0 / D) + NORM_EPS)
    norm_ref[...] = (res_ref[c] * scale * gain_ref[c]).astype(BF16)

    def finish():
        swap_copy.wait_send()
        each(1, devices, lambda j: ctx_copy(j).wait_send())
        each(1, chips, lambda j: part_copy(j).wait_send())

    return finish


def add(ref, *others):
    if len(ref.shape) > 2:
        for i in range(ref.shape[0]):
            add(ref.at[i], *[o.at[i] for o in others])
        return
    value = ref[...].astype(F32)
    for o in others:
        value = value + o[...].astype(F32)
    ref[...] = value.astype(BF16)


class Ring4:
    def __init__(self, post, block, into, pos, lo, hi, to):
        self.post, self.block, self.into, self.lo, self.hi = post, block, into, lo, hi
        self.pos, self.plus, self.minus, self.far_at = pos, step(pos, 1, 4), step(pos, -1, 4), step(pos, 2, 4)
        self.up, self.down = to(1), to(-1)

    def put(self, src, i, device):
        return self.post.put(src, self.into.at[i], device, self.into.at[i])

    def far(self):
        self.far_up = self.put(self.block(self.far_at, self.lo), 0, self.up)
        self.far_down = self.put(self.block(self.far_at, self.hi), 1, self.down)

    def near(self):
        self.free_up = self.put(self.block(self.plus, self.hi), 2, self.up)
        self.free_down = self.put(self.block(self.minus, self.lo), 3, self.down)

    def last(self):
        self.far_up()
        add(self.block(self.plus, self.lo), self.into.at[0])
        self.last_up = self.put(self.block(self.plus, self.lo), 4, self.up)
        self.far_down()
        add(self.block(self.minus, self.hi), self.into.at[1])
        self.last_down = self.put(self.block(self.minus, self.hi), 5, self.down)

    def finish(self):
        self.free_up()
        self.last_down()
        add(self.block(self.pos, self.hi), self.into.at[2], self.into.at[5])
        self.free_down()
        self.last_up()
        add(self.block(self.pos, self.lo), self.into.at[3], self.into.at[4])


def ring8(post, sums, into, z, y, x, c):
    up_to, down_to = dev(step(z, 1, NZ), y, x, c), dev(step(z, -1, NZ), y, x, c)
    count = 0

    def half(dz, h):
        return sums.at[step(z, dz, NZ), pl.ds(2 * h, 2)]

    def put(dz, h):
        nonlocal count
        i = count
        count += 1
        return post.put(half(dz, h), into.at[i], up_to if dz > 0 else down_to, into.at[i]), into.at[i]

    up, down = [None, None], [None, None]
    up[0] = put(4, 0)
    down[1] = post.put(half(4, 1), into.at[count], down_to, into.at[count]), into.at[count]
    count += 1
    up[1], down[0] = put(3, 1), put(-3, 0)
    yield
    for dz in (3, 2, 1):
        for h_up in (0, 1):
            reach = dz if h_up == 0 else dz - 1
            if reach == 0:
                continue
            h_down = 1 - h_up
            up[h_up][0]()
            add(half(reach, h_up), up[h_up][1])
            up[h_up] = put(reach, h_up)
            down[h_down][0]()
            add(half(-reach, h_down), down[h_down][1])
            down[h_down] = put(-reach, h_down)
            yield
    for h in (1, 0):
        up[h][0]()
        down[h][0]()
        add(sums.at[z, pl.ds(2 * h, 2)], up[h][1], down[h][1])


SUM_AB, SUM_C = 1536, 1024


def moe_part(
    post, norm_ref, ids_ref, gates_ref, out_ref,
    block_ab, block_c, g, gate_up, down, hidden, other, from_other, sums, other_c, from_c, sums_c,
    ring_a, ring_b, ring_c, ring_d, ring_z, row_in, block_in, z_in, final, loads, local_sem,
):
    z, y, x, c = here()
    lane = lax.broadcasted_iota(jnp.int32, (4, TABLE), 1)
    ids, gates = ids_ref[...], gates_ref[...].astype(F32)
    table = sum(jnp.where(ids[:, k : k + 1] == lane, gates[:, k : k + 1], 0.0) for k in range(ids.shape[1]))
    block_ab[...] = norm_ref[:, : Tokens.AB]
    block_c[:, : HALF - Tokens.AB] = norm_ref[:, Tokens.AB :]
    block_c[:, HALF - Tokens.AB :] = both_halves(table, c).astype(BF16)
    for _ in gather(post, (block_ab, block_c), Tokens(g), local_sem):
        pass
    for load in loads:
        load.wait()

    e = (y * NX + x) * 2 + c
    ours = (lax.broadcasted_iota(jnp.int32, (256, TABLE), 1) == e).astype(F32)

    def hidden_rows(i, carry):
        rows = [g[h, i].reshape(256, HALF + TABLE) for h in range(2)]
        weight = jnp.sum(
            (rows[0][:, HALF:].astype(F32) + rows[1][:, HALF:].astype(F32)) * ours, axis=1, keepdims=True
        )
        product = sum(
            lax.dot_general(
                rows[h][:, :HALF], gate_up[:, h * HALF : (h + 1) * HALF], (((1,), (1,)), ((), ())),
                preferred_element_type=F32,
            )
            for h in range(2)
        )
        gated, raised = product[:, :FFG], product[:, FFG:]
        hidden[i] = (gated / (1.0 + jnp.exp(-gated)) * raised * weight).astype(BF16).reshape(NX, 64, FFG)
        return carry

    lax.fori_loop(0, NY, hidden_rows, 0)

    xs = [step(x, o, NX) for o in range(NX)]
    ys = [step(y, o, NY) for o in range(NY)]
    tile = SUM_AB // 2
    twin = dev(z, y, x, 1 - c)

    def place(ref, name, o):
        if name == "a":
            return ref.at[ys[o], :, pl.ds(0, 32)]
        return ref.at[:, xs[o], pl.ds(32, 32)]

    def rows_of(name, o):
        return place(hidden, name, o)[...].reshape(128, FFG)

    def columns_c(i, rows):
        return jnp.dot(rows, down[i, :, SUM_AB:], preferred_element_type=F32).reshape(NX, NZ, 8, SUM_C)

    arrive = {}

    def give(name, o):
        rows = rows_of(name, o)
        for i in range(2):
            columns = pl.ds(i * tile, tile)
            part = jnp.dot(rows, down[1, :, columns], preferred_element_type=F32)
            place(other, name, o).at[:, :, columns][...] = part.reshape(4, 32, tile).astype(BF16)
        arrive[(name, o)] = post.put(place(other, name, o), place(from_other, name, o), twin, place(from_other, name, o))

    def take(name, o):
        arrive[(name, o)]()
        rows = rows_of(name, o)
        for i in range(2):
            columns = pl.ds(i * tile, tile)
            part = jnp.dot(rows, down[0, :, columns], preferred_element_type=F32).reshape(4, 32, tile)
            theirs = place(from_other, name, o).at[:, :, columns][...].astype(F32)
            place(sums, name, o).at[:, :, columns][...] = (part + theirs).astype(BF16)

    def give_c(i, carry):
        part = columns_c(1, hidden[i].reshape(256, FFG))
        for xx in range(NX):
            other_c[:, i, xx] = part[xx].astype(BF16)
        return carry

    def take_c(i, carry):
        part = columns_c(0, hidden[i].reshape(256, FFG))
        for xx in range(NX):
            sums_c[:, i, xx] = (part[xx] + from_c[:, i, xx].astype(F32)).astype(BF16)
        return carry

    a_lo, a_hi, b_lo, b_hi = [pl.ds(16 * i, 16) for i in range(4)]

    def to_x(s):
        return dev(z, y, step(x, s, NX), c)

    def to_y(s):
        return dev(z, step(y, s, NY), x, c)

    first = (
        Ring4(post, lambda p, r: sums.at[p, :, r], ring_a, y, a_lo, a_hi, to_y),
        Ring4(post, lambda p, r: sums.at[:, p, r], ring_b, x, b_lo, b_hi, to_x),
    )
    second = (
        Ring4(post, lambda p, r: sums.at[y, p, r], ring_c, x, a_lo, a_hi, to_x),
        Ring4(post, lambda p, r: sums.at[p, x, r], ring_d, y, b_lo, b_hi, to_y),
    )
    along_z = ring8(post, sums_c, ring_z, z, y, x, c)

    lax.fori_loop(0, NY, give_c, 0)
    arrive_c = post.put(other_c, from_c, twin, from_c)
    give("a", 2)
    give("b", 2)
    arrive_c()
    lax.fori_loop(0, NY, take_c, 0)
    next(along_z)
    take("a", 2)
    take("b", 2)
    for ring in first:
        ring.far()
    for o in (1, 3):
        give("a", o)
        give("b", o)
    next(along_z)
    for o in (1, 3):
        take("a", o)
        take("b", o)
    for ring in first:
        ring.near()
    give("a", 0)
    give("b", 0)
    next(along_z)
    for ring in first:
        ring.last()
    take("a", 0)
    take("b", 0)
    next(along_z)
    for ring in first:
        ring.finish()
    for ring in second:
        ring.far()
        ring.near()
    next(along_z)
    for ring in second:
        ring.last()
    next(along_z)
    for ring in second:
        ring.finish()

    def zrows(at):
        return pl.ds(pl.multiple_of(at * 8, 8), 8)

    waits = [
        post.put(sums.at[y, x, zrows(step(z, j, NZ))], z_in.at[j], dev(step(z, j, NZ), y, x, c), z_in.at[j])
        for j in (1, 7, 2, 6, 3, 5, 4)
    ]
    keep = pltpu.make_async_copy(sums.at[y, x, zrows(z)], z_in.at[0], local_sem.at[0])
    keep.start()
    for _ in along_z:
        pass
    row_waits = [
        post.put(sums_c.at[z, step(y, o, NY)], row_in.at[o], to_y(o), row_in.at[o]) for o in (1, 3, 2)
    ]
    for wait in row_waits:
        wait()
    add(sums_c.at[z, y], *[row_in.at[o] for o in (1, 2, 3)])
    block_waits = [
        post.put(sums_c.at[z, y, step(x, o, NX)], block_in.at[o], to_x(o), block_in.at[o]) for o in (1, 3, 2)
    ]
    keep.wait()
    for wait in waits:
        wait()
    value = z_in[0].astype(F32)
    for j in range(1, NZ):
        value = value + z_in[j].astype(F32)
    final[c, :, :SUM_AB] = value
    for wait in block_waits:
        wait()
    value = sums_c[z, y, x].astype(F32)
    for o in range(1, 4):
        value = value + block_in[o].astype(F32)
    final[c, :, SUM_AB:] = value
    post.put(final.at[c], final.at[c], twin, final.at[1 - c])()
    own_rows(out_ref, final, c)


def layer_kernel(
    q_ref, own_ref, block_ab_ref, block_c_ref, list_ref, prefix_ref, suffix_ref,
    value_up_ref, hidden_ref, gain_ref, ids_ref, gates_ref, proj_hbm, gate_hbm, up_hbm, down_hbm,
    res_ref, out_ref,
    pool_ab, pool_c, top, total, acc, ctx,
    ctx_in, proj, p_other, p_from, parts, parts_in, full, residual, normed,
    block_ab, block_c, g, gate_up, down, hidden, other, from_other, sums, other_c, from_c, sums_c,
    ring_a, ring_b, ring_c, ring_d, ring_z, row_in, block_in, z_in, final,
    send, recv, local_sem, load_sem, ctx_send, ctx_recv, part_send, part_recv, sib_send, sib_recv,
):
    z, y, x, c = here()
    devices = 2 * NX * NY
    e = (y * NX + x) * 2 + c

    def column_half(half):
        return pl.ds(pl.multiple_of(half * HALF, 128), HALF)

    pairs = [(proj_hbm.at[:, column_half(half)], proj.at[i]) for i, half in enumerate((c, 1 - c))]
    pairs += [(gate_hbm.at[0], gate_up.at[pl.ds(0, FFG)]), (up_hbm.at[0], gate_up.at[pl.ds(FFG, FFG)])]
    pairs += [(down_hbm.at[0, :, column_half(half)], down.at[i]) for i, half in enumerate((c, 1 - c))]
    loads = [pltpu.make_async_copy(src, dst, load_sem.at[i]) for i, (src, dst) in enumerate(pairs)]
    for load in loads:
        load.start()

    barrier = pltpu.get_barrier_semaphore()

    def hello(j, carry):
        pl.semaphore_signal(
            barrier, inc=1, device_id=(z, lax.rem(e + j, devices)), device_id_type=MESH
        )
        return carry

    lax.fori_loop(1, devices, hello, 0)
    for j in range(1, NZ):
        pl.semaphore_signal(barrier, inc=1, device_id=dev(step(z, j, NZ), y, x, c), device_id_type=MESH)
    pl.semaphore_wait(barrier, devices - 1 + NZ - 1)

    post = Post(send, recv)
    attend_part(
        post, q_ref, own_ref, block_ab_ref, block_c_ref, list_ref, prefix_ref, suffix_ref, ctx,
        pool_ab, pool_c, top, total, acc, local_sem,
    )
    finish = project_part(
        ctx, value_up_ref, hidden_ref, gain_ref, normed,
        ctx_in, proj, p_other, p_from, parts, parts_in, full, residual, loads[:2],
        local_sem.at[0], ctx_send, ctx_recv, part_send, part_recv, sib_send, sib_recv,
    )
    moe_part(
        post, normed, ids_ref, gates_ref, out_ref,
        block_ab, block_c, g, gate_up, down, hidden, other, from_other, sums, other_c, from_c, sums_c,
        ring_a, ring_b, ring_c, ring_d, ring_z, row_in, block_in, z_in, final, loads[2:], local_sem,
    )
    own_rows(res_ref, residual, c)
    finish()
    post.drain()


def layer(*operands):
    vmem = pl.BlockSpec(memory_space=pltpu.VMEM)
    hbm = pl.BlockSpec(memory_space=pl.ANY)
    chips, rows = NX * NY, 256
    return pl.pallas_call(
        layer_kernel,
        out_shape=(jax.ShapeDtypeStruct((4, D), F32), jax.ShapeDtypeStruct((4, D), F32)),
        in_specs=[vmem] * 5 + [pl.BlockSpec(memory_space=pltpu.SMEM)] * 2 + [vmem] * 5 + [hbm] * 4,
        out_specs=(vmem, vmem),
        scratch_shapes=[
            pltpu.VMEM((2, NY, NX, NZ, Pool.AB, KDIM), BF16),
            pltpu.VMEM((2, NZ, Pool.C, KDIM), BF16),
            pltpu.VMEM((rows, 1), F32),
            pltpu.VMEM((rows, 1), F32),
            pltpu.VMEM((rows, LAT), F32),
            pltpu.VMEM((2 * chips, 8, LAT), BF16),
            pltpu.VMEM((2 * chips, 8, LAT), BF16),
            pltpu.VMEM((2, 256, HALF), BF16),
            pltpu.VMEM((chips, 8, HALF), BF16),
            pltpu.VMEM((chips, 8, HALF), BF16),
            pltpu.VMEM((chips, 8, HALF), BF16),
            pltpu.VMEM((chips, 8, HALF), BF16),
            pltpu.VMEM((chips, 8, HALF), F32),
            pltpu.VMEM((2, 8, HALF), F32),
            pltpu.VMEM((8, HALF), BF16),
            pltpu.VMEM((8, Tokens.AB), BF16),
            pltpu.VMEM((8, Tokens.C), BF16),
            pltpu.VMEM((2, NY, NX, NZ * 8, HALF + TABLE), BF16),
            pltpu.VMEM((2 * FFG, D), BF16),
            pltpu.VMEM((2, FFG, HALF), BF16),
            pltpu.VMEM((NY, NX, 64, FFG), BF16),
            pltpu.VMEM((NY, NX, 64, SUM_AB), BF16),
            pltpu.VMEM((NY, NX, 64, SUM_AB), BF16),
            pltpu.VMEM((NY, NX, 64, SUM_AB), BF16),
            pltpu.VMEM((NZ, NY, NX, 8, SUM_C), BF16),
            pltpu.VMEM((NZ, NY, NX, 8, SUM_C), BF16),
            pltpu.VMEM((NZ, NY, NX, 8, SUM_C), BF16),
            pltpu.VMEM((6, NX, 16, SUM_AB), BF16),
            pltpu.VMEM((6, NY, 16, SUM_AB), BF16),
            pltpu.VMEM((6, 16, SUM_AB), BF16),
            pltpu.VMEM((6, 16, SUM_AB), BF16),
            pltpu.VMEM((14, NY // 2, NX, 8, SUM_C), BF16),
            pltpu.VMEM((4, NX, 8, SUM_C), BF16),
            pltpu.VMEM((4, 8, SUM_C), BF16),
            pltpu.VMEM((NZ, 8, SUM_AB), BF16),
            pltpu.VMEM((2, 8, HALF), F32),
            pltpu.SemaphoreType.DMA((COPIES,)),
            pltpu.SemaphoreType.DMA((COPIES,)),
            pltpu.SemaphoreType.DMA((2,)),
            pltpu.SemaphoreType.DMA((6,)),
            pltpu.SemaphoreType.DMA((2 * chips,)),
            pltpu.SemaphoreType.DMA((2 * chips,)),
            pltpu.SemaphoreType.DMA((chips,)),
            pltpu.SemaphoreType.DMA((chips,)),
            pltpu.SemaphoreType.DMA((2,)),
            pltpu.SemaphoreType.DMA((2,)),
        ],
        compiler_params=pltpu.CompilerParams(
            collective_id=0, has_side_effects=True, vmem_limit_bytes=60 * 2**20
        ),
        name="layer",
    )(*operands)


def per_device(
    hidden_in, query, prefix_pool, suffix_cache, block_list, prefix_count, suffix_count, value_up,
    out_proj, norm_gain, expert_ids, gate_weights, gate_proj, up_proj, down_proj,
):
    e = lax.axis_index("expert")
    core, chip = lax.rem(e, 2), lax.div(e, 2)

    block_ab = lax.dynamic_slice(prefix_pool, (chip, core * (24 * KDIM)), (1, 24 * KDIM)).reshape(1, 24, KDIM)
    block_c = lax.dynamic_slice(prefix_pool, (core * 8, 48 * KDIM), (8, 16 * KDIM)).reshape(128, KDIM)
    q = query.reshape(4, 32, 2, KDIM).transpose(1, 2, 0, 3).reshape(256, KDIM)
    own = suffix_cache.reshape(4 * SUFFIX, KDIM)
    return layer(
        q, own, block_ab, block_c, block_list, prefix_count, suffix_count,
        value_up, hidden_in, norm_gain.astype(F32).reshape(2, 1, HALF), expert_ids, gate_weights,
        out_proj, gate_proj.transpose(0, 2, 1), up_proj.transpose(0, 2, 1), down_proj,
    )


def solution(mesh):
    rows = P(("dp", "expert"), None)
    in_specs = (
        rows, rows, P("dp", None), rows, rows, P(("dp", "expert")), P(("dp", "expert")),
        P("expert", None, None), P("expert", None), P(), rows, rows,
        P("expert", None, "dp"), P("expert", None, "dp"), P("expert", "dp", None),
    )
    return jax.shard_map(
        per_device, mesh=mesh, in_specs=in_specs, out_specs=(rows, rows), check_vma=False
    )
```

```python
import functools
import jax
import jax.numpy as jnp
from jax import lax
from jax.experimental import pallas as pl
from jax.experimental.pallas import tpu as pltpu
from jax.sharding import PartitionSpec as P

HEADS = 64
LAT = 512
BLOCK = 64
SUFFIX = 128
KDIM = 576
D = 5120
HALF = 2560
FFG = 192
TABLE = 128

NEG_FILL = -1e30
SCORE_SCALE = 192.0 ** (-0.5)
NORM_EPS = 1e-06
LOG2_E = 1.4426950408889634

NX, NY, NZ = 4, 4, 8
MESH = pl.DeviceIdType.MESH
F32 = jnp.float32
BF16 = jnp.bfloat16


def here():
    z = lax.axis_index("dp")
    e = lax.axis_index("expert")
    core = lax.rem(e, 2)
    chip = lax.div(e, 2)
    return z, lax.div(chip, NX), lax.rem(chip, NX), core


def dev(z, y, x, core):
    return (z, (y * NX + x) * 2 + core)


def step(v, by, n):
    return lax.rem(v + by + n, n)


class Post:
    def __init__(self, send, recv):
        self.send, self.recv, self.count, self.sent = send, recv, 0, []

    def put(self, src, dst, to, lands):
        i = self.count
        self.count += 1
        copy = pltpu.make_async_remote_copy(
            src_ref=src, dst_ref=dst, send_sem=self.send.at[i], recv_sem=self.recv.at[i],
            device_id=to, device_id_type=MESH,
        )
        copy.start()
        self.sent.append(copy)
        return pltpu.make_async_remote_copy(
            src_ref=lands, dst_ref=lands, send_sem=self.send.at[i], recv_sem=self.recv.at[i],
            device_id=to, device_id_type=MESH,
        ).wait_recv

    def drain(self):
        for copy in self.sent:
            copy.wait_send()


def gather(post, block, g, local_sem):
    z, y, x, c = here()
    xs = {o: step(x, o, NX) for o in (0, -1, 1, 2)}
    ys = {o: step(y, o, NY) for o in (0, -1, 1, 2)}
    zs = {o: step(z, o, NZ) for o in range(-4, 5)}
    other = dev(z, y, x, 1 - c)

    def move(view, arriving, to):
        return post.put(view, view, to, arriving)

    block_ab, block_c = block
    whole = g.c_block is None
    keeps = [
        pltpu.make_async_copy(block_ab, g.ab(c, y, x, z, 1), local_sem.at[0]),
        pltpu.make_async_copy(block_c, g.c_slab(c, z) if whole else g.c_block(c, y, x, z), local_sem.at[1]),
    ]
    for keep in keeps:
        keep.start()
    c_x = [] if whole else [
        post.put(block_c, g.c_block(c, y, x, z), dev(z, y, step(x, o, NX), c), g.c_block(c, y, step(x, -o, NX), z))
        for o in (1, 3, 2)
    ]
    ab_z = [
        post.put(block_ab, g.ab(c, y, x, z, 1), dev(step(z, j, NZ), y, x, c), g.ab(c, y, x, step(z, -j, NZ), 1))
        for j in (1, 7, 2, 6, 3, 5, 4)
    ]
    for keep in keeps:
        keep.wait()
    from_sibling = {}

    def sibling_c(dz):
        from_sibling[dz] = move(g.c_slab(c, zs[dz]), g.c_slab(1 - c, zs[dz]), other)

    def along_z(dz, by, part):
        return move(g.c_slab(c, zs[dz], part), g.c_slab(c, zs[dz - by], part), dev(zs[by], y, x, c))

    up, down = {}, {}

    def begin_z():
        for part in range(PARTS):
            up[part], down[PARTS - 1 - part] = along_z(0, 1, part), along_z(0, -1, PARTS - 1 - part)
        sibling_c(0)

    ring_events = [(s, part) for s in (1, 2, 3) for part in range(PARTS)]

    def ring_z(events):
        for _ in range(events):
            s, part = ring_events.pop(0)
            up[part]()
            if s < 3 or part < PARTS // 2:
                up[part] = along_z(-s, 1, part)
            back = PARTS - 1 - part
            down[back]()
            if s < 3 or back >= PARTS // 2:
                down[back] = along_z(s, -1, back)
            if part == PARTS - 1:
                sibling_c(-s)
                sibling_c(s)

    for wait in c_x:
        wait()
    c_y = [] if whole else [
        move(g.c_row(c, y, z), g.c_row(c, step(y, -o, NY), z), dev(z, step(y, o, NY), x, c)) for o in (1, 3, 2)
    ]
    if whole:
        begin_z()
    yield []
    for wait in ab_z:
        wait()

    halves = {"a": (0, 4), "b": (4, 4), "a_lo": (0, 2), "a_hi": (2, 2), "b_lo": (4, 2), "b_hi": (6, 2)}
    def sibling(name, dy, dx):
        yy, xx = ys[dy], xs[dx]
        from_sibling[(name, dy, dx)] = move(g.ab(c, yy, xx, *halves[name]), g.ab(1 - c, yy, xx, *halves[name]), other)

    def along_x(dy, dx, name, by):
        yy, xx = ys[dy], xs[dx]
        return move(
            g.ab(c, yy, xx, *halves[name]), g.ab(c, yy, step(xx, -by, NX), *halves[name]), dev(z, y, xs[by], c)
        )

    def along_y(dy, dx, name, by):
        yy, xx = ys[dy], xs[dx]
        return move(
            g.ab(c, yy, xx, *halves[name]), g.ab(c, step(yy, -by, NY), xx, *halves[name]), dev(z, ys[by], x, c)
        )

    a1p, b1p = along_x(0, 0, "a", 1), along_y(0, 0, "b", 1)
    a1m, b1m = along_x(0, 0, "a", -1), along_y(0, 0, "b", -1)
    sibling("a", 0, 0)
    sibling("b", 0, 0)
    a2, b2 = {}, {}

    def second(o):
        a2[o] = (along_y(0, o, "a", 1), along_y(0, o, "a", -1))
        b2[o] = (along_x(o, 0, "b", 1), along_x(o, 0, "b", -1))

    second(0)
    if not whole:
        for wait in c_y:
            wait()
        begin_z()
    else:
        ring_z(PARTS)
    a1p()
    fa_lo = along_x(0, -1, "a_lo", 1)
    b1p()
    fb_lo = along_y(-1, 0, "b_lo", 1)
    a1m()
    fa_hi = along_x(0, 1, "a_hi", -1)
    b1m()
    fb_hi = along_y(1, 0, "b_hi", -1)
    for o in (-1, 1):
        second(o)
        sibling("a", 0, o)
        sibling("b", o, 0)

    def done(*parts):
        ready = []
        for part in parts:
            if isinstance(part, int):
                from_sibling[part]()
                ready.append((zs[part],))
            else:
                from_sibling[("a",) + part]()
                from_sibling[("b",) + part]()
                ready.append((ys[part[0]], xs[part[1]]))
        return ready

    queue = [(0, 0), 0]

    def some():
        return done(queue.pop(0)) if queue else []

    yield some()
    ring_z(PARTS)
    yield some()
    fa_lo()
    fa_hi()
    fb_lo()
    fb_hi()
    second(2)
    sibling("a", 0, 2)
    sibling("b", 2, 0)

    last_a, last_b = {}, {}
    ready = {
        0: [(-1, 0), (1, 0), (0, -1), (0, 1)], -1: [(-1, -1)], 1: [(1, 1), (1, -1), (-1, 1)], 2: [],
    }
    seen = 0
    for o in (0, -1, 1, 2):
        ring_z(min(PARTS // 2, len(ring_events)))
        yield some()
        a2[o][0]()
        lo_a = along_y(-1, o, "a_lo", 1)
        b2[o][0]()
        lo_b = along_x(o, -1, "b_lo", 1)
        yield some()
        a2[o][1]()
        last_a[o] = (lo_a, along_y(1, o, "a_hi", -1))
        b2[o][1]()
        last_b[o] = (lo_b, along_x(o, 1, "b_hi", -1))
        for side in (-1, 1):
            sibling("a", side, o)
            sibling("b", o, side)
        yield some()
        now = 3 - -(-len(ring_events) // PARTS)
        queue += ready[o] + [d for n in range(seen + 1, now + 1) for d in (-n, n)]
        seen = now
    for o in (0, -1, 1, 2):
        for wait in last_a[o]:
            wait()
        sibling("a", 2, o)
        yield some()
        for wait in last_b[o]:
            wait()
        sibling("b", o, 2)
        yield some()
        queue += [(2, o), (o, 2)] if o != 2 else [(2, 2)]
    for part in range(PARTS // 2):
        up[part]()
        down[PARTS - 1 - part]()
    sibling_c(4)
    queue += [4]
    while queue:
        yield some()


COPIES = 400
PARTS = 4


class Pool:
    AB, C = 24, 128
    c_block = None

    def __init__(self, ab, c):
        self.g_ab, self.g_c = ab, c

    def ab(self, core, yy, xx, z0, nz):
        return self.g_ab.at[core, yy, xx, pl.ds(z0, nz)]

    def c_slab(self, core, zz, part=None):
        if part is None:
            return self.g_c.at[core, zz]
        return self.g_c.at[core, zz, pl.ds(part * (self.C // PARTS), self.C // PARTS)]


class Tokens:
    AB, C = 1792, 896

    def __init__(self, g):
        self.g = g

    def rows(self, z0, nz):
        return pl.ds(pl.multiple_of(z0 * 8, 8), nz * 8)

    def ab(self, core, yy, xx, z0, nz):
        return self.g.at[core, yy, xx, self.rows(z0, nz), pl.ds(0, self.AB)]

    def c_block(self, core, yy, xx, zz):
        return self.g.at[core, yy, xx, self.rows(zz, 1), pl.ds(self.AB, self.C)]

    def c_row(self, core, yy, zz):
        return self.g.at[core, yy, :, self.rows(zz, 1), pl.ds(self.AB, self.C)]

    def c_slab(self, core, zz, part=None):
        ys = pl.ds(0, NY) if part is None else pl.ds(part * (NY // PARTS), NY // PARTS)
        return self.g.at[core, ys, :, self.rows(zz, 1), pl.ds(self.AB, self.C)]


def attend_part(
    post, q_ref, own_ref, block_ab_ref, block_c_ref, list_ref, prefix_ref, suffix_ref, out_ref,
    g_ab, g_c, top, total, acc, local_sem,
):
    def request(shape):
        return lax.rem(lax.broadcasted_iota(jnp.int32, shape, 0), 4)

    def by_request(ref, shape):
        turn = request(shape)
        return jnp.where(turn == 0, ref[0], jnp.where(turn == 1, ref[1], jnp.where(turn == 2, ref[2], ref[3])))

    def live_bias(live):
        return (live.astype(F32) - 1.0) * -NEG_FILL

    def member_blocks():
        listed = jnp.concatenate([list_ref[...], list_ref[...]], axis=0)
        block, count = lax.broadcasted_iota(jnp.int32, (8, 128), 1), by_request(prefix_ref, (8, 128))
        member = jnp.zeros((8, 128), F32)
        for j in range(listed.shape[1]):
            member = jnp.where((listed[:, j : j + 1] == block) & (j < count), 1.0, member)
        return member.astype(BF16)

    def own_bias():
        shape = (8, 4 * SUFFIX)
        row = lax.broadcasted_iota(jnp.int32, shape, 1)
        place = row - SUFFIX * request(shape)
        return live_bias(jnp.where((place >= 0) & (place < by_request(suffix_ref, shape)), 1.0, 0.0))

    def pool_bias(member, block_of_key):
        block = lax.broadcasted_iota(jnp.int32, (128, block_of_key.shape[1]), 0)
        spread = jnp.where(block == block_of_key, 1.0, 0.0).astype(BF16)
        return live_bias(jnp.dot(member, spread, preferred_element_type=F32))

    def ab_bias(member, k):
        key = lax.broadcasted_iota(jnp.int32, (1, 2 * NZ * Pool.AB), 1)
        zz = sum((key >= Pool.AB * i).astype(jnp.int32) for i in range(1, 2 * NZ))
        return pool_bias(member, (zz - jnp.where(zz >= NZ, NZ, 0)) * 16 + k)

    def c_bias(member, zz):
        key = lax.broadcasted_iota(jnp.int32, (1, 2 * Pool.C), 1)
        return pool_bias(member, lax.shift_right_logical(key, 4) + zz * 16)

    def merge(keys, bias, first=False):
        q = q_ref[...]
        scores = lax.dot_general(q, keys, (((1,), (1,)), ((), ())), preferred_element_type=F32)
        rows, width = scores.shape
        scores = (scores.reshape(rows // 8, 8, width) * (SCORE_SCALE * LOG2_E) + bias[None]).reshape(rows, width)
        best = jnp.max(scores, axis=1, keepdims=True)
        if not first:
            best = jnp.maximum(best, top[...])
        weights = jnp.exp2(scores - best)
        summed = jnp.sum(weights, axis=1, keepdims=True)
        mixed = jnp.dot(weights.astype(BF16), keys[:, :LAT], preferred_element_type=F32)
        if first:
            total[...] = summed
            acc[...] = mixed
        else:
            scale = jnp.exp2(top[...] - best)
            total[...] = total[...] * scale + summed
            acc[...] = acc[...] * scale + mixed
        top[...] = best

    pool = Pool(g_ab, g_c)
    block = block_ab_ref, block_c_ref
    started = False
    for parts in gather(post, block, pool, local_sem):
        if not started:
            merge(own_ref[...], own_bias(), first=True)
            member = member_blocks()
            started = True
        for part in parts:
            if len(part) == 2:
                yy, xx = part
                keys = jnp.concatenate([g_ab[h, yy, xx].reshape(NZ * Pool.AB, KDIM) for h in range(2)], axis=0)
                merge(keys, ab_bias(member, yy * NX + xx))
            else:
                keys = jnp.concatenate([g_c[0, part[0]], g_c[1, part[0]]], axis=0)
                merge(keys, c_bias(member, part[0]))
    out_ref[...] = (acc[...] / total[...]).reshape(out_ref.shape).astype(BF16)


def both_halves(v, c):
    v = jnp.concatenate([v, v], axis=0)
    return jnp.where(lax.broadcasted_iota(jnp.int32, v.shape, 0) // 4 == c, v, 0.0)


def own_rows(out_ref, halves, c):
    upper = lax.broadcasted_iota(jnp.int32, (4, HALF), 0) * 0 + c == 0
    for h in range(2):
        out_ref[:, h * HALF : (h + 1) * HALF] = jnp.where(upper, halves[h, :4], halves[h, 4:])


def project_part(
    ctx_ref, up_ref, hidden_ref, gain_ref, norm_ref,
    ctx_in, proj, other, from_other, parts, parts_in, full, res_ref, loads,
    local_sem, ctx_send, ctx_recv, send, recv, sib_send, sib_recv,
):
    z, y, x, c = here()
    e = (y * NX + x) * 2 + c
    chip = y * NX + x
    devices = 2 * NX * NY
    chips = NX * NY

    def ctx_copy(j):
        to = lax.rem(e + j, devices)
        return pltpu.make_async_remote_copy(
            src_ref=ctx_ref.at[to], dst_ref=ctx_in.at[e], send_sem=ctx_send.at[j], recv_sem=ctx_recv.at[j],
            device_id=(z, to), device_id_type=MESH,
        )

    def ctx_arrival(j):
        source = lax.rem(e - j + devices, devices)
        return pltpu.make_async_remote_copy(
            src_ref=ctx_in.at[source], dst_ref=ctx_in.at[source], send_sem=ctx_send.at[j],
            recv_sem=ctx_recv.at[j], device_id=(z, source), device_id_type=MESH,
        )

    def each(low, high, act):
        def body(j, carry):
            act(j)
            return carry

        lax.fori_loop(low, high, body, 0)

    each(1, devices, lambda j: ctx_copy(j).start())
    mine = pltpu.make_async_copy(ctx_ref.at[e], ctx_in.at[e], local_sem)
    mine.start()
    mine.wait()
    for load in loads:
        load.wait()
    each(1, devices, lambda j: ctx_arrival(j).wait_recv())

    context = ctx_in[...].reshape(devices * 8, LAT)
    first = jnp.dot(context, up_ref[0], preferred_element_type=F32).reshape(chips, 16, 128)
    second = jnp.dot(context, up_ref[1], preferred_element_type=F32).reshape(chips, 16, 128)
    upper = lax.broadcasted_iota(jnp.int32, (chips, 8, 128), 1) < 4

    def swap(v):
        return jnp.concatenate([v[:, 4:], v[:, :4]], axis=1)

    left = jnp.where(upper, first[:, :8], swap(first[:, 8:]))
    right = jnp.where(upper, swap(second[:, :8]), second[:, 8:])
    values = jnp.concatenate([left, right], axis=2).reshape(chips * 8, 256).astype(BF16)

    tile = 640
    for i in range(HALF // tile):
        columns = pl.ds(i * tile, tile)
        part = jnp.dot(values, proj[1, :, columns], preferred_element_type=F32)
        other[:, :, columns] = part.reshape(chips, 8, tile).astype(BF16)
    hidden = both_halves(hidden_ref[...].astype(F32), c)
    first_half = lax.broadcasted_iota(jnp.int32, (8, HALF), 0) * 0 + c == 0
    hidden_own = jnp.where(first_half, hidden[:, :HALF], hidden[:, HALF:])
    hidden_other = jnp.where(first_half, hidden[:, HALF:], hidden[:, :HALF])
    other[chip] = (other[chip].astype(F32) + hidden_other).astype(BF16)
    sib = pltpu.make_async_remote_copy(
        src_ref=other, dst_ref=from_other, send_sem=sib_send.at[0], recv_sem=sib_recv.at[0],
        device_id=dev(z, y, x, 1 - c), device_id_type=MESH,
    )
    sib.start()
    for i in range(HALF // tile):
        columns = pl.ds(i * tile, tile)
        part = jnp.dot(values, proj[0, :, columns], preferred_element_type=F32)
        full[:, :, columns] = part.reshape(chips, 8, tile)
    sib.wait()

    def part_copy(j):
        to = lax.rem(chip + j, chips)
        return pltpu.make_async_remote_copy(
            src_ref=parts.at[to], dst_ref=parts_in.at[j], send_sem=send.at[j], recv_sem=recv.at[j],
            device_id=(z, to * 2 + c), device_id_type=MESH,
        )

    def give_part(j):
        to = lax.rem(chip + j, chips)
        parts[to] = (full[to] + from_other[to].astype(F32)).astype(BF16)
        part_copy(j).start()

    each(1, chips, give_part)
    full[chip] = full[chip] + from_other[chip].astype(F32)
    res_ref[c] = full[chip] + hidden_own
    each(1, chips, lambda j: part_copy(j).wait_recv())

    def gathered(j, carry):
        return carry + parts_in[j].astype(F32)

    res_ref[c] = lax.fori_loop(1, chips, gathered, res_ref[c])
    swap_copy = pltpu.make_async_remote_copy(
        src_ref=res_ref.at[c], dst_ref=res_ref.at[c], send_sem=sib_send.at[1], recv_sem=sib_recv.at[1],
        device_id=dev(z, y, x, 1 - c), device_id_type=MESH,
    )
    swap_copy.start()
    swap_in = pltpu.make_async_remote_copy(
        src_ref=res_ref.at[1 - c], dst_ref=res_ref.at[1 - c], send_sem=sib_send.at[1],
        recv_sem=sib_recv.at[1], device_id=dev(z, y, x, 1 - c), device_id_type=MESH,
    )
    swap_in.wait_recv()
    squares = sum(jnp.sum(res_ref[h] * res_ref[h], axis=1, keepdims=True) for h in range(2))
    scale = lax.rsqrt(squares * (1.0 / D) + NORM_EPS)
    norm_ref[...] = (res_ref[c] * scale * gain_ref[c]).astype(BF16)

    def finish():
        swap_copy.wait_send()
        each(1, devices, lambda j: ctx_copy(j).wait_send())
        each(1, chips, lambda j: part_copy(j).wait_send())

    return finish


def add(ref, *others):
    if len(ref.shape) > 2:
        for i in range(ref.shape[0]):
            add(ref.at[i], *[o.at[i] for o in others])
        return
    value = ref[...].astype(F32)
    for o in others:
        value = value + o[...].astype(F32)
    ref[...] = value.astype(BF16)


class Ring4:
    def __init__(self, post, block, into, pos, lo, hi, to):
        self.post, self.block, self.into, self.lo, self.hi = post, block, into, lo, hi
        self.pos, self.plus, self.minus, self.far_at = pos, step(pos, 1, 4), step(pos, -1, 4), step(pos, 2, 4)
        self.up, self.down = to(1), to(-1)

    def put(self, src, i, device):
        return self.post.put(src, self.into.at[i], device, self.into.at[i])

    def far(self):
        self.far_up = self.put(self.block(self.far_at, self.lo), 0, self.up)
        self.far_down = self.put(self.block(self.far_at, self.hi), 1, self.down)

    def near(self):
        self.free_up = self.put(self.block(self.plus, self.hi), 2, self.up)
        self.free_down = self.put(self.block(self.minus, self.lo), 3, self.down)

    def last(self):
        self.far_up()
        add(self.block(self.plus, self.lo), self.into.at[0])
        self.last_up = self.put(self.block(self.plus, self.lo), 4, self.up)
        self.far_down()
        add(self.block(self.minus, self.hi), self.into.at[1])
        self.last_down = self.put(self.block(self.minus, self.hi), 5, self.down)

    def finish(self):
        self.free_up()
        self.last_down()
        add(self.block(self.pos, self.hi), self.into.at[2], self.into.at[5])
        self.free_down()
        self.last_up()
        add(self.block(self.pos, self.lo), self.into.at[3], self.into.at[4])


def ring8(post, sums, into, z, y, x, c):
    up_to, down_to = dev(step(z, 1, NZ), y, x, c), dev(step(z, -1, NZ), y, x, c)
    count = 0

    def half(dz, h):
        return sums.at[step(z, dz, NZ), pl.ds(2 * h, 2)]

    def put(dz, h):
        nonlocal count
        i = count
        count += 1
        return post.put(half(dz, h), into.at[i], up_to if dz > 0 else down_to, into.at[i]), into.at[i]

    up, down = [None, None], [None, None]
    up[0] = put(4, 0)
    down[1] = post.put(half(4, 1), into.at[count], down_to, into.at[count]), into.at[count]
    count += 1
    up[1], down[0] = put(3, 1), put(-3, 0)
    yield
    for dz in (3, 2, 1):
        for h_up in (0, 1):
            reach = dz if h_up == 0 else dz - 1
            if reach == 0:
                continue
            h_down = 1 - h_up
            up[h_up][0]()
            add(half(reach, h_up), up[h_up][1])
            up[h_up] = put(reach, h_up)
            down[h_down][0]()
            add(half(-reach, h_down), down[h_down][1])
            down[h_down] = put(-reach, h_down)
            yield
    for h in (1, 0):
        up[h][0]()
        down[h][0]()
        add(sums.at[z, pl.ds(2 * h, 2)], up[h][1], down[h][1])


SUM_AB, SUM_C = 1792, 768


def moe_part(
    post, norm_ref, ids_ref, gates_ref, out_ref,
    block_ab, block_c, g, gate_up, down, hidden, other, from_other, sums, other_c, from_c, sums_c,
    ring_a, ring_b, ring_c, ring_d, ring_z, row_in, block_in, z_in, final, product_ab, loads, local_sem,
):
    z, y, x, c = here()
    lane = lax.broadcasted_iota(jnp.int32, (4, TABLE), 1)
    ids, gates = ids_ref[...], gates_ref[...].astype(F32)
    table = sum(jnp.where(ids[:, k : k + 1] == lane, gates[:, k : k + 1], 0.0) for k in range(ids.shape[1]))
    block_ab[...] = norm_ref[:, : Tokens.AB]
    block_c[:, : HALF - Tokens.AB] = norm_ref[:, Tokens.AB :]
    block_c[:, HALF - Tokens.AB :] = both_halves(table, c).astype(BF16)
    columns_ab = [pl.ds(h * HALF, Tokens.AB) for h in range(2)]
    columns_rest = [pl.ds(h * HALF + Tokens.AB, HALF - Tokens.AB) for h in range(2)]

    def times(rows, columns):
        return lax.dot_general(rows, gate_up[:, columns], (((1,), (1,)), ((), ())), preferred_element_type=F32)

    chunks = []
    for parts in gather(post, (block_ab, block_c), Tokens(g), local_sem):
        chunks += [part for part in parts if len(part) == 2]
        if len(chunks) == 4:
            if loads:
                for load in loads:
                    load.wait()
                loads = []
            part = sum(
                times(jnp.concatenate([g[h, yy, xx, :, : Tokens.AB] for yy, xx in chunks], axis=0), columns_ab[h])
                for h in range(2)
            )
            for i, (yy, xx) in enumerate(chunks):
                product_ab[yy, xx] = part[i * 64 : (i + 1) * 64]
            chunks = []

    e = (y * NX + x) * 2 + c
    ours = (lax.broadcasted_iota(jnp.int32, (256, TABLE), 1) == e).astype(F32)

    def hidden_rows(i, carry):
        rows = [g[h, i, :, :, Tokens.AB :].reshape(256, Tokens.C) for h in range(2)]
        rest = HALF - Tokens.AB
        weight = jnp.sum(
            (rows[0][:, rest:].astype(F32) + rows[1][:, rest:].astype(F32)) * ours, axis=1, keepdims=True
        )
        product = product_ab[i].reshape(256, 2 * FFG)
        for h in range(2):
            product = product + times(rows[h][:, :rest], columns_rest[h])
        gated, raised = product[:, :FFG], product[:, FFG:]
        hidden[i] = (gated / (1.0 + jnp.exp(-gated)) * raised * weight).astype(BF16).reshape(NX, 64, FFG)
        return carry

    lax.fori_loop(0, NY, hidden_rows, 0)

    xs = [step(x, o, NX) for o in range(NX)]
    ys = [step(y, o, NY) for o in range(NY)]
    tile = SUM_AB // 2
    twin = dev(z, y, x, 1 - c)

    def place(ref, name, o):
        if name == "a":
            return ref.at[ys[o], :, pl.ds(0, 32)]
        return ref.at[:, xs[o], pl.ds(32, 32)]

    def rows_of(name, o):
        return place(hidden, name, o)[...].reshape(128, FFG)

    def columns_c(i, rows):
        return jnp.dot(rows, down[i, :, SUM_AB:], preferred_element_type=F32).reshape(NX, NZ, 8, SUM_C)

    arrive = {}

    def give(name, o):
        rows = rows_of(name, o)
        for i in range(2):
            columns = pl.ds(i * tile, tile)
            part = jnp.dot(rows, down[1, :, columns], preferred_element_type=F32)
            place(other, name, o).at[:, :, columns][...] = part.reshape(4, 32, tile).astype(BF16)
        arrive[(name, o)] = post.put(place(other, name, o), place(from_other, name, o), twin, place(from_other, name, o))

    def take(name, o):
        arrive[(name, o)]()
        rows = rows_of(name, o)
        for i in range(2):
            columns = pl.ds(i * tile, tile)
            part = jnp.dot(rows, down[0, :, columns], preferred_element_type=F32).reshape(4, 32, tile)
            theirs = place(from_other, name, o).at[:, :, columns][...].astype(F32)
            place(sums, name, o).at[:, :, columns][...] = (part + theirs).astype(BF16)

    def give_c(i, carry):
        part = columns_c(1, hidden[i].reshape(256, FFG))
        for xx in range(NX):
            other_c[:, i, xx] = part[xx].astype(BF16)
        return carry

    def take_c(i, carry):
        part = columns_c(0, hidden[i].reshape(256, FFG))
        for xx in range(NX):
            sums_c[:, i, xx] = (part[xx] + from_c[:, i, xx].astype(F32)).astype(BF16)
        return carry

    a_lo, a_hi, b_lo, b_hi = [pl.ds(16 * i, 16) for i in range(4)]

    def to_x(s):
        return dev(z, y, step(x, s, NX), c)

    def to_y(s):
        return dev(z, step(y, s, NY), x, c)

    first = (
        Ring4(post, lambda p, r: sums.at[p, :, r], ring_a, y, a_lo, a_hi, to_y),
        Ring4(post, lambda p, r: sums.at[:, p, r], ring_b, x, b_lo, b_hi, to_x),
    )
    second = (
        Ring4(post, lambda p, r: sums.at[y, p, r], ring_c, x, a_lo, a_hi, to_x),
        Ring4(post, lambda p, r: sums.at[p, x, r], ring_d, y, b_lo, b_hi, to_y),
    )
    along_z = ring8(post, sums_c, ring_z, z, y, x, c)

    lax.fori_loop(0, NY, give_c, 0)
    arrive_c = post.put(other_c, from_c, twin, from_c)
    give("a", 2)
    give("b", 2)
    arrive_c()
    lax.fori_loop(0, NY, take_c, 0)
    next(along_z)
    take("a", 2)
    take("b", 2)
    for ring in first:
        ring.far()
    for o in (1, 3):
        give("a", o)
        give("b", o)
    next(along_z)
    for o in (1, 3):
        take("a", o)
        take("b", o)
    for ring in first:
        ring.near()
    give("a", 0)
    give("b", 0)
    next(along_z)
    for ring in first:
        ring.last()
    take("a", 0)
    take("b", 0)
    next(along_z)
    for ring in first:
        ring.finish()
    for ring in second:
        ring.far()
        ring.near()
    next(along_z)
    for ring in second:
        ring.last()
    next(along_z)
    for ring in second:
        ring.finish()

    def zrows(at):
        return pl.ds(pl.multiple_of(at * 8, 8), 8)

    waits = [
        post.put(sums.at[y, x, zrows(step(z, j, NZ))], z_in.at[j], dev(step(z, j, NZ), y, x, c), z_in.at[j])
        for j in (1, 7, 2, 6, 3, 5, 4)
    ]
    keep = pltpu.make_async_copy(sums.at[y, x, zrows(z)], z_in.at[0], local_sem.at[0])
    keep.start()
    for _ in along_z:
        pass
    row_waits = [
        post.put(sums_c.at[z, step(y, o, NY)], row_in.at[o], to_y(o), row_in.at[o]) for o in (1, 3, 2)
    ]
    for wait in row_waits:
        wait()
    add(sums_c.at[z, y], *[row_in.at[o] for o in (1, 2, 3)])
    block_waits = [
        post.put(sums_c.at[z, y, step(x, o, NX)], block_in.at[o], to_x(o), block_in.at[o]) for o in (1, 3, 2)
    ]
    keep.wait()
    for wait in waits:
        wait()
    value = z_in[0].astype(F32)
    for j in range(1, NZ):
        value = value + z_in[j].astype(F32)
    final[c, :, :SUM_AB] = value
    for wait in block_waits:
        wait()
    value = sums_c[z, y, x].astype(F32)
    for o in range(1, 4):
        value = value + block_in[o].astype(F32)
    final[c, :, SUM_AB:] = value
    post.put(final.at[c], final.at[c], twin, final.at[1 - c])()
    own_rows(out_ref, final, c)


def layer_kernel(
    q_ref, own_ref, block_ab_ref, block_c_ref, list_ref, prefix_ref, suffix_ref,
    value_up_ref, hidden_ref, gain_ref, ids_ref, gates_ref, proj_hbm, gate_hbm, up_hbm, down_hbm,
    res_ref, out_ref,
    pool_ab, pool_c, top, total, acc, ctx,
    ctx_in, proj, p_other, p_from, parts, parts_in, full, residual, normed,
    block_ab, block_c, g, gate_up, down, hidden, other, from_other, sums, other_c, from_c, sums_c,
    ring_a, ring_b, ring_c, ring_d, ring_z, row_in, block_in, z_in, final, product_ab,
    send, recv, local_sem, load_sem, ctx_send, ctx_recv, part_send, part_recv, sib_send, sib_recv,
):
    z, y, x, c = here()
    devices = 2 * NX * NY
    e = (y * NX + x) * 2 + c

    def column_half(half):
        return pl.ds(pl.multiple_of(half * HALF, 128), HALF)

    pairs = [(proj_hbm.at[:, column_half(half)], proj.at[i]) for i, half in enumerate((c, 1 - c))]
    pairs += [(gate_hbm.at[0], gate_up.at[pl.ds(0, FFG)]), (up_hbm.at[0], gate_up.at[pl.ds(FFG, FFG)])]
    pairs += [(down_hbm.at[0, :, column_half(half)], down.at[i]) for i, half in enumerate((c, 1 - c))]
    loads = [pltpu.make_async_copy(src, dst, load_sem.at[i]) for i, (src, dst) in enumerate(pairs)]
    for load in loads:
        load.start()

    barrier = pltpu.get_barrier_semaphore()

    def hello(j, carry):
        pl.semaphore_signal(
            barrier, inc=1, device_id=(z, lax.rem(e + j, devices)), device_id_type=MESH
        )
        return carry

    lax.fori_loop(1, devices, hello, 0)
    for j in range(1, NZ):
        pl.semaphore_signal(barrier, inc=1, device_id=dev(step(z, j, NZ), y, x, c), device_id_type=MESH)
    pl.semaphore_wait(barrier, devices - 1 + NZ - 1)

    post = Post(send, recv)
    attend_part(
        post, q_ref, own_ref, block_ab_ref, block_c_ref, list_ref, prefix_ref, suffix_ref, ctx,
        pool_ab, pool_c, top, total, acc, local_sem,
    )
    finish = project_part(
        ctx, value_up_ref, hidden_ref, gain_ref, normed,
        ctx_in, proj, p_other, p_from, parts, parts_in, full, residual, loads[:2],
        local_sem.at[0], ctx_send, ctx_recv, part_send, part_recv, sib_send, sib_recv,
    )
    moe_part(
        post, normed, ids_ref, gates_ref, out_ref,
        block_ab, block_c, g, gate_up, down, hidden, other, from_other, sums, other_c, from_c, sums_c,
        ring_a, ring_b, ring_c, ring_d, ring_z, row_in, block_in, z_in, final, product_ab, loads[2:], local_sem,
    )
    own_rows(res_ref, residual, c)
    finish()
    post.drain()


def layer(*operands):
    vmem = pl.BlockSpec(memory_space=pltpu.VMEM)
    hbm = pl.BlockSpec(memory_space=pl.ANY)
    chips, rows = NX * NY, 256
    return pl.pallas_call(
        layer_kernel,
        out_shape=(jax.ShapeDtypeStruct((4, D), F32), jax.ShapeDtypeStruct((4, D), F32)),
        in_specs=[vmem] * 5 + [pl.BlockSpec(memory_space=pltpu.SMEM)] * 2 + [vmem] * 5 + [hbm] * 4,
        out_specs=(vmem, vmem),
        scratch_shapes=[
            pltpu.VMEM((2, NY, NX, NZ, Pool.AB, KDIM), BF16),
            pltpu.VMEM((2, NZ, Pool.C, KDIM), BF16),
            pltpu.VMEM((rows, 1), F32),
            pltpu.VMEM((rows, 1), F32),
            pltpu.VMEM((rows, LAT), F32),
            pltpu.VMEM((2 * chips, 8, LAT), BF16),
            pltpu.VMEM((2 * chips, 8, LAT), BF16),
            pltpu.VMEM((2, 256, HALF), BF16),
            pltpu.VMEM((chips, 8, HALF), BF16),
            pltpu.VMEM((chips, 8, HALF), BF16),
            pltpu.VMEM((chips, 8, HALF), BF16),
            pltpu.VMEM((chips, 8, HALF), BF16),
            pltpu.VMEM((chips, 8, HALF), F32),
            pltpu.VMEM((2, 8, HALF), F32),
            pltpu.VMEM((8, HALF), BF16),
            pltpu.VMEM((8, Tokens.AB), BF16),
            pltpu.VMEM((8, Tokens.C), BF16),
            pltpu.VMEM((2, NY, NX, NZ * 8, HALF + TABLE), BF16),
            pltpu.VMEM((2 * FFG, D), BF16),
            pltpu.VMEM((2, FFG, HALF), BF16),
            pltpu.VMEM((NY, NX, 64, FFG), BF16),
            pltpu.VMEM((NY, NX, 64, SUM_AB), BF16),
            pltpu.VMEM((NY, NX, 64, SUM_AB), BF16),
            pltpu.VMEM((NY, NX, 64, SUM_AB), BF16),
            pltpu.VMEM((NZ, NY, NX, 8, SUM_C), BF16),
            pltpu.VMEM((NZ, NY, NX, 8, SUM_C), BF16),
            pltpu.VMEM((NZ, NY, NX, 8, SUM_C), BF16),
            pltpu.VMEM((6, NX, 16, SUM_AB), BF16),
            pltpu.VMEM((6, NY, 16, SUM_AB), BF16),
            pltpu.VMEM((6, 16, SUM_AB), BF16),
            pltpu.VMEM((6, 16, SUM_AB), BF16),
            pltpu.VMEM((14, NY // 2, NX, 8, SUM_C), BF16),
            pltpu.VMEM((4, NX, 8, SUM_C), BF16),
            pltpu.VMEM((4, 8, SUM_C), BF16),
            pltpu.VMEM((NZ, 8, SUM_AB), BF16),
            pltpu.VMEM((2, 8, HALF), F32),
            pltpu.VMEM((NY, NX, 64, 2 * FFG), F32),
            pltpu.SemaphoreType.DMA((COPIES,)),
            pltpu.SemaphoreType.DMA((COPIES,)),
            pltpu.SemaphoreType.DMA((2,)),
            pltpu.SemaphoreType.DMA((6,)),
            pltpu.SemaphoreType.DMA((2 * chips,)),
            pltpu.SemaphoreType.DMA((2 * chips,)),
            pltpu.SemaphoreType.DMA((chips,)),
            pltpu.SemaphoreType.DMA((chips,)),
            pltpu.SemaphoreType.DMA((2,)),
            pltpu.SemaphoreType.DMA((2,)),
        ],
        compiler_params=pltpu.CompilerParams(
            collective_id=0, has_side_effects=True, vmem_limit_bytes=60 * 2**20
        ),
        name="layer",
    )(*operands)


def per_device(
    hidden_in, query, prefix_pool, suffix_cache, block_list, prefix_count, suffix_count, value_up,
    out_proj, norm_gain, expert_ids, gate_weights, gate_proj, up_proj, down_proj,
):
    e = lax.axis_index("expert")
    core, chip = lax.rem(e, 2), lax.div(e, 2)

    block_ab = lax.dynamic_slice(prefix_pool, (chip, core * (24 * KDIM)), (1, 24 * KDIM)).reshape(1, 24, KDIM)
    block_c = lax.dynamic_slice(prefix_pool, (core * 8, 48 * KDIM), (8, 16 * KDIM)).reshape(128, KDIM)
    q = query.reshape(4, 32, 2, KDIM).transpose(1, 2, 0, 3).reshape(256, KDIM)
    own = suffix_cache.reshape(4 * SUFFIX, KDIM)
    return layer(
        q, own, block_ab, block_c, block_list, prefix_count, suffix_count,
        value_up, hidden_in, norm_gain.astype(F32).reshape(2, 1, HALF), expert_ids, gate_weights,
        out_proj, gate_proj.transpose(0, 2, 1), up_proj.transpose(0, 2, 1), down_proj,
    )


def solution(mesh):
    rows = P(("dp", "expert"), None)
    in_specs = (
        rows, rows, P("dp", None), rows, rows, P(("dp", "expert")), P(("dp", "expert")),
        P("expert", None, None), P("expert", None), P(), rows, rows,
        P("expert", None, "dp"), P("expert", None, "dp"), P("expert", "dp", None),
    )
    return jax.shard_map(
        per_device, mesh=mesh, in_specs=in_specs, out_specs=(rows, rows), check_vma=False
    )
```
